32 devices in a mesh: row: 8 (over z, core), col: 4 (over y, x).
Axes of the slice: x: 2, y: 2, z: 4, core: 2. Of those that a mesh axis runs over, the one named last changes fastest.
Arguments:
- codes: int32 [256, 256], P('row', 'col'), may hold values from 0 to 511
- starts: int32 [256], replicated, may hold values from 0 to 255, as said below
- embed: bfloat16 [512, 512], replicated, may hold values from -6 to 6
- gain_one: float32 [512], replicated, may hold values from 0.1 to 1.9
- row_qkv: bfloat16 [512, 1536], replicated, may hold values from -2 to 2
- row_out: bfloat16 [512, 512], replicated, may hold values from -0.25 to 0.25
- gain_two: float32 [512], replicated, may hold values from 0.1 to 1.9
- col_qkv: bfloat16 [512, 640], replicated, may hold values from -2 to 2
- col_out: bfloat16 [512, 512], replicated, may hold values from -0.25 to 0.25
- gain_three: float32 [512], replicated, may hold values from 0.1 to 1.9
- mlp_in: bfloat16 [512, 1024], replicated, may hold values from -0.25 to 0.25
- mlp_out: bfloat16 [1024, 512], replicated, may hold values from -0.1875 to 0.1875
- project: bfloat16 [512, 128], replicated, may hold values from -0.25 to 0.25
- conv_one: bfloat16 [3, 3, 128, 128], replicated, may hold values from -0.1875 to 0.1875
- conv_two: bfloat16 [3, 3, 128, 128], replicated, may hold values from -0.1875 to 0.1875
Outputs:
- block_out: float32 [256, 256, 512], P('row', 'col')
- image: float32 [512, 512, 128], P('row', 'col')
The draws below stay inside these ranges and needn't reach their ends.
Inputs may be any that keep to these rules, and one draw needn't show every extreme that they name: starts[i] is at most i.
All inputs are finite; a program needn't handle non-finite values.
Results may differ from the reference program's by a relative error of at most 0.013.
The reference program's roundings to bfloat16 on the way count: a program that leaves them out, or rounds other values in their place, can miss the bound.
Values may be sent and summed in bfloat16 or wider, within the bound.
No kernel may reach another device: no remote copies, remote signals or barrier semaphores. Data moves between devices by JAX's collectives and lax.ppermute only.
A program may use at most 192 MiB of HBM per device.

```python
import math
import jax
import jax.numpy as jnp
import numpy as np
from jax import lax

D = 512
HEADS = 8
FF = 1024
VOCAB = 512
CW = 128
COL_DEV = 64
HD = 64
NR = 256
NC = 256


def draw_starts(key, part):
    limits = jnp.arange(NR, dtype=jnp.int32) + 1
    return jax.random.randint(key, (NR,), 0, limits, dtype=jnp.int32)


def draw_row_qkv(key, part):
    key_q, key_k, key_v = jax.random.split(key, 3)
    scale = D ** (-0.5)
    base_q = jax.random.normal(key_q, (D, D), jnp.float32) * scale
    base_k = jax.random.normal(key_k, (D, D), jnp.float32) * scale
    base_v = jax.random.normal(key_v, (D, D), jnp.float32) * scale
    queries = base_q
    keys = base_k
    return jnp.clip(jnp.concatenate([queries, keys, base_v], axis=1), -2.0, 2.0).astype(jnp.bfloat16)


def draw_col_qkv(key, part):
    key_q, key_k, key_v = jax.random.split(jax.random.fold_in(key, 7), 3)
    scale = D ** (-0.5)
    base_q = jax.random.normal(key_q, (D, D), jnp.float32) * scale
    base_k = jax.random.normal(key_k, (D, HD), jnp.float32) * scale
    base_v = jax.random.normal(key_v, (D, HD), jnp.float32) * scale
    queries = base_q
    keys = base_k
    return jnp.clip(jnp.concatenate([queries, keys, base_v], axis=1), -2.0, 2.0).astype(jnp.bfloat16)


def with_ends(values, own_key, least, top_value):
    longest = values.shape.index(max(values.shape))
    spots = []
    for shift in (0, 1):
        where = [jax.random.randint(jax.random.fold_in(own_key, axis), (), 0, length) for axis, length in enumerate(values.shape)]
        where[longest] = (where[longest] + shift) % values.shape[longest]
        spots.append(tuple(where))
    return values.at[spots[0]].set(least).at[spots[1]].set(top_value)


def cumulative_ranks(number_of, skew):
    loads = [(1 << 20) // math.isqrt(rank ** skew) + 1 for rank in range(1, number_of + 1)]
    spread = 1 + sum(loads) // (1 << 30)
    return np.cumsum(np.array([max(1, weight // spread) for weight in loads]))


def skewed_ids(stream_key, extent, count, lean):
    table = cumulative_ranks(count, lean)
    pick = jax.random.randint(jax.random.fold_in(stream_key, 1), extent, 0, int(table[count - 1]))
    rank = jnp.searchsorted(jnp.asarray(table, jnp.int32), pick, side="right")
    return jax.random.permutation(jax.random.fold_in(stream_key, 2), count)[rank].astype(jnp.int32)


def normal_values(rng, extent, spread, reach, kind=jnp.bfloat16):
    values = spread * jax.random.normal(rng, extent, jnp.float32)
    return jnp.clip(values, min=-reach, max=reach).astype(kind)


def setup_inputs(seed: int = 0) -> dict:
    seeds = jax.random.split(jax.random.key(seed), 16)
    return {
        "codes": with_ends(skewed_ids(seeds[0], (NR, NC), VOCAB, 1), jax.random.fold_in(seeds[0], 3), 0, VOCAB - 1).astype(jnp.int32),
        "starts": draw_starts(jax.random.fold_in(seeds[15], 71), 0),
        "embed": normal_values(seeds[2], (VOCAB, D), 1.0, 6.0),
        "gain_one": jnp.clip(1.0 + 0.18 * jax.random.normal(seeds[3], (D,), jnp.float32), 0.1, 1.9),
        "row_qkv": draw_row_qkv(jax.random.fold_in(seeds[15], 71), 0),
        "row_out": normal_values(seeds[5], (D, D), D ** -0.5, 0.25),
        "gain_two": jnp.clip(1.0 + 0.18 * jax.random.normal(seeds[6], (D,), jnp.float32), 0.1, 1.9),
        "col_qkv": draw_col_qkv(jax.random.fold_in(seeds[15], 71), 0),
        "col_out": normal_values(seeds[8], (D, D), D ** -0.5, 0.25),
        "gain_three": jnp.clip(1.0 + 0.18 * jax.random.normal(seeds[9], (D,), jnp.float32), 0.1, 1.9),
        "mlp_in": normal_values(seeds[10], (D, FF), D ** -0.5, 0.25),
        "mlp_out": normal_values(seeds[11], (FF, D), FF ** -0.5, 0.1875),
        "project": normal_values(seeds[12], (D, CW), D ** -0.5, 0.25),
        "conv_one": normal_values(seeds[13], (3, 3, CW, CW), (9 * CW) ** -0.5, 0.1875),
        "conv_two": normal_values(seeds[14], (3, 3, CW, CW), (9 * CW) ** -0.5, 0.1875),
    }


EPS = 1e-06
NEGATIVE = -1e+30

def norm_round(values, norm_gain):
    scale = lax.rsqrt(lax.optimization_barrier(jnp.mean(values * values, axis=-1, keepdims=True)) + EPS)
    return (values * scale * norm_gain).astype(jnp.bfloat16)

def matmul(left, right):
    return jnp.einsum('...i,ij->...j', left.astype(jnp.float32), right.astype(jnp.float32))

def softmax_round(scores, visible):
    scores = jnp.where(visible, scores, NEGATIVE)
    top = lax.optimization_barrier(jnp.max(scores, axis=-1, keepdims=True))
    raised = jnp.exp(scores - top)
    return (raised / lax.optimization_barrier(jnp.sum(raised, axis=-1, keepdims=True))).astype(jnp.bfloat16)

def row_attend(queries, keys, values, head_count, first_column):
    depth = queries.shape[0]
    query_len = queries.shape[1]
    key_len = keys.shape[1]
    head_size = queries.shape[2] // head_count
    query_cols = first_column + jnp.arange(query_len, dtype=jnp.int32)
    key_cols = jnp.arange(key_len, dtype=jnp.int32)
    visible = query_cols[:, None] >= key_cols[None, :]

    def split_heads(block, length):
        return jnp.moveaxis(block.reshape(depth, length, head_count, head_size), 2, 0)

    def one_head(parts):
        head_q, head_k, head_v = parts
        scores = jnp.einsum('rqd,rkd->rqk', head_q.astype(jnp.float32), head_k.astype(jnp.float32)) * head_size ** (-0.5)
        soft_weights = softmax_round(scores, visible)
        return jnp.einsum('rqk,rkd->rqd', soft_weights.astype(jnp.float32), head_v.astype(jnp.float32)).astype(jnp.bfloat16)
    mixed = lax.map(one_head, (split_heads(queries, query_len), split_heads(keys, key_len), split_heads(values, key_len)))
    return jnp.moveaxis(mixed, 0, 2).reshape(depth, query_len, head_count * head_size)

def col_attend(queries, key_value, query_rows, query_starts):
    row_len, column_count, feature_width = queries.shape
    key_len = key_value.shape[0]
    head_size = key_value.shape[2] // 2
    head_count = feature_width // head_size
    split = queries.reshape(row_len, column_count, head_count, head_size)
    keys = key_value[..., :head_size]
    values = key_value[..., head_size:]
    scores = jnp.einsum('qchd,kcd->chqk', split.astype(jnp.float32), keys.astype(jnp.float32)) * head_size ** (-0.5)
    key_rows = jnp.arange(key_len, dtype=jnp.int32)
    visible = (key_rows[None, :] <= query_rows[:, None]) & (key_rows[None, :] >= query_starts[:, None])
    soft_weights = softmax_round(scores, visible)
    mixed = jnp.einsum('chqk,kcd->qchd', soft_weights.astype(jnp.float32), values.astype(jnp.float32)).astype(jnp.bfloat16)
    return mixed.reshape(row_len, column_count, feature_width)

def upsample(grid):
    return jnp.repeat(jnp.repeat(grid, 2, axis=0), 2, axis=1)

def conv_three(padded, kernel):
    height = padded.shape[0] - 2
    breadth = padded.shape[1] - 2
    total = jnp.zeros((height, breadth, kernel.shape[3]), jnp.float32)
    for shift_down in range(3):
        for shift_right in range(3):
            window = padded[shift_down:shift_down + height, shift_right:shift_right + breadth]
            total = total + matmul(window, kernel[shift_down, shift_right])
    return total

def pad_grid(grid):
    return jnp.pad(grid, ((1, 1), (1, 1), (0, 0)))

def reference(codes, starts, embed, gain_one, row_qkv, row_out, gain_two, col_qkv, col_out, gain_three, mlp_in, mlp_out, project, conv_one, conv_two):
    vocab_ids = jnp.arange(VOCAB, dtype=jnp.int32)
    one_hot = (codes[..., None] == vocab_ids).astype(jnp.bfloat16)
    hidden = matmul(one_hot, embed)
    normed = norm_round(hidden, gain_one)
    projected = matmul(normed, row_qkv).astype(jnp.bfloat16)
    queries = projected[..., :D]
    keys = projected[..., D:2 * D]
    values = projected[..., 2 * D:]

    def one_row(parts):
        return row_attend(parts[0][None], parts[1][None], parts[2][None], HEADS, 0)[0]
    row_mixed = lax.map(one_row, (queries, keys, values))
    hidden = hidden + matmul(row_mixed, row_out)
    normed = norm_round(hidden, gain_two)
    projected = matmul(normed, col_qkv).astype(jnp.bfloat16)
    col_queries = projected[..., :D]
    key_value = projected[..., D:]
    block_count = NC // COL_DEV

    def to_blocks(grid):
        return jnp.moveaxis(grid.reshape(NR, block_count, COL_DEV, grid.shape[2]), 1, 0)
    all_rows = jnp.arange(NR, dtype=jnp.int32)

    def one_block(parts):
        return col_attend(parts[0], parts[1], all_rows, starts)
    col_mixed = lax.map(one_block, (to_blocks(col_queries), to_blocks(key_value)))
    col_mixed = jnp.moveaxis(col_mixed, 0, 1).reshape(NR, NC, D)
    hidden = hidden + matmul(col_mixed, col_out)
    normed = norm_round(hidden, gain_three)
    inner = jax.nn.silu(matmul(normed, mlp_in)).astype(jnp.bfloat16)
    block_out = hidden + matmul(inner, mlp_out)
    coarse = matmul(block_out.astype(jnp.bfloat16), project).astype(jnp.bfloat16)
    upsampled = upsample(coarse)
    first = jax.nn.silu(conv_three(pad_grid(upsampled), conv_one)).astype(jnp.bfloat16)
    image = upsampled.astype(jnp.float32) + conv_three(pad_grid(first), conv_two)
    return (block_out, image)
```

```python
import functools
import jax
import jax.numpy as jnp
from jax import lax
from jax.experimental import pallas as pl
from jax.experimental.pallas import tpu as pltpu
from jax.sharding import PartitionSpec as P

HEADS = 8
CHUNKS = 2
EPS = 1e-06
NEGATIVE = -1e30
BF = jnp.bfloat16
F32 = jnp.float32
VM = pl.BlockSpec(memory_space=pltpu.VMEM)
SM = pl.BlockSpec(memory_space=pltpu.SMEM)
PARAMS = pltpu.CompilerParams(vmem_limit_bytes=56 * 1024 * 1024)


def dot(left, right):
    return jnp.dot(left, right, preferred_element_type=F32)


def dot_t(left, right):
    return lax.dot_general(left, right, (((1,), (1,)), ((), ())), preferred_element_type=F32)


def norm_round(values, norm_gain):
    scale = lax.rsqrt(jnp.mean(values * values, axis=-1, keepdims=True) + EPS)
    return (values * scale * norm_gain).astype(BF)


def silu(values):
    return values / (1.0 + jnp.exp(-values))


def one_hot(ids, vocab):
    ids = jnp.concatenate([ids] * (vocab // ids.shape[1]), axis=1)
    spots = lax.broadcasted_iota(jnp.int32, ids.shape, 1)
    spots = (spots - vocab // 2).astype(F32).astype(BF)
    return jnp.where(ids == spots, jnp.ones_like(ids), jnp.zeros_like(ids))


def low_half(shape):
    return lax.broadcasted_iota(jnp.int32, shape, len(shape) - 1) % 128 < 64


def row_kernel(
    bias_ref,
    key_ids_ref,
    row_ids_ref,
    col_ids_ref,
    query_table_ref,
    pair_table_ref,
    embed_ref,
    row_out_ref,
    gain_ref,
    col_qkv_ref,
    hidden_ref,
    query_ref,
    pair_ref,
    mixed_ref,
    queries_ref,
):
    rows, keys = key_ids_ref.shape
    vocab, width = query_table_ref.shape
    cols = bias_ref.shape[0]
    tiles = width // 128
    queries_ref[...] = dot(one_hot(row_ids_ref[...], vocab), query_table_ref[...]).astype(BF)
    spots = lax.broadcasted_iota(jnp.int32, (vocab, keys), 0)
    spots = (spots - vocab // 2).astype(F32).astype(BF)
    low = low_half((cols, 128))
    ones = jnp.ones((128, keys), BF)

    def one_row(row, carry):
        ids = key_ids_ref[pl.ds(row, 1), :].astype(BF)
        ids = jnp.broadcast_to(ids, (vocab, keys))
        chosen = jnp.where(ids == spots, jnp.ones_like(ids), jnp.zeros_like(ids))
        pairs = dot(pair_table_ref[...], chosen).astype(BF)
        bias = bias_ref[...]
        bias = jnp.concatenate([bias, bias], axis=0)
        for tile in range(tiles):
            lanes = slice(tile * 128, (tile + 1) * 128)
            query = queries_ref[pl.ds(row * cols, cols), lanes]
            none = jnp.zeros_like(query)
            query = jnp.concatenate([jnp.where(low, query, none), jnp.where(low, none, query)], axis=0)
            scores = dot(query, pairs[lanes, :]) + bias
            raised = jnp.exp(scores - jnp.max(scores, axis=1, keepdims=True)).astype(BF)
            value = pairs[width + tile * 128 : width + (tile + 1) * 128, :]
            found = dot_t(raised, jnp.concatenate([value, ones], axis=0))
            found = found[:, :128] / found[:, 128:]
            mixed_ref[tile, pl.ds(row, cols, stride=rows), :] = jnp.where(low, found[:cols], found[cols:])
        return carry

    lax.fori_loop(0, rows, one_row, 0, unroll=2)

    step = 256

    def tail(block, carry):
        here = pl.ds(pl.multiple_of(block * step, step), step)
        mixed = jnp.concatenate([mixed_ref[tile, here, :].astype(BF) for tile in range(tiles)], axis=1)
        hidden = dot(one_hot(col_ids_ref[here, :], vocab), embed_ref[...])
        hidden = hidden + dot(mixed, row_out_ref[...])
        hidden_ref[here, :] = hidden
        projected = dot(norm_round(hidden, gain_ref[...]), col_qkv_ref[...]).astype(BF)
        query_ref[here, :] = projected[:, :width] * jnp.asarray((width // HEADS) ** (-0.5), BF)
        pair_ref[here, :] = projected[:, width:]
        return carry

    lax.fori_loop(0, rows * cols // step, tail, 0)


def row_stage(bias, key_ids, row_ids, col_ids, query_table, pair_table, embed, row_out, gain, col_qkv):
    rows = key_ids.shape[0]
    cols = bias.shape[0]
    cells = rows * cols
    width = embed.shape[1]
    return pl.pallas_call(
        row_kernel,
        out_shape=(
            jax.ShapeDtypeStruct((cells, width), F32),
            jax.ShapeDtypeStruct((cells, width), BF),
            jax.ShapeDtypeStruct((cells, col_qkv.shape[1] - width), BF),
        ),
        in_specs=[VM] * 10,
        out_specs=(VM, VM, VM),
        scratch_shapes=[
            pltpu.VMEM((width // 128, cells, 128), F32),
            pltpu.VMEM((cells, width), BF),
        ],
        compiler_params=PARAMS,
        name="row_stage",
    )(bias, key_ids, row_ids, col_ids, query_table, pair_table, embed, row_out, gain, col_qkv)


def col_kernel(chunks, blocks, *refs):
    queries = refs[:chunks]
    hiddens = refs[chunks : 2 * chunks]
    pairs = refs[2 * chunks : 2 * chunks + blocks]
    (
        bias_ref,
        col_out_ref,
        gain_ref,
        mlp_in_ref,
        mlp_out_ref,
        project_ref,
        block_ref,
        coarse_ref,
        wide_ref,
        thin_ref,
        mixed_ref,
    ) = refs[2 * chunks + blocks :]
    group = queries[0].shape[0]
    rows = queries[0].shape[1] * chunks
    width = queries[0].shape[2]
    tiles = width // 128
    keys = bias_ref.shape[1]
    low = low_half((rows, 128))
    low_keys = low_half((keys, 128))
    bias = jnp.concatenate([bias_ref[...]] * tiles, axis=0)

    def one_column(column, carry):
        query = jnp.concatenate([part[column] for part in queries], axis=0)
        none = jnp.zeros((rows, 128), BF)
        evens, odds = [], []
        for tile in range(tiles):
            piece = query[:, tile * 128 : (tile + 1) * 128]
            evens.append(jnp.where(low, piece, none))
            odds.append(jnp.where(low, none, piece))
        pair = jnp.concatenate([part[column] for part in pairs], axis=0)
        turned = jnp.concatenate([pair[:, 64:], pair[:, :64]], axis=1)
        ones = jnp.ones((keys, 128), BF)
        founds = []
        for pieces, key, value in (
            (evens, pair, jnp.where(low_keys, turned, ones)),
            (odds, turned, jnp.where(low_keys, ones, pair)),
        ):
            scores = dot_t(jnp.concatenate(pieces, axis=0), key) + bias
            raised = jnp.exp(scores - jnp.max(scores, axis=1, keepdims=True)).astype(BF)
            founds.append(dot(raised, value))
        for tile in range(tiles):
            here = slice(tile * rows, (tile + 1) * rows)
            even, odd = founds[0][here], founds[1][here]
            total = pltpu.roll(jnp.where(low, odd, even), 64, 1)
            mixed = jnp.where(low, even, odd) / total
            mixed_ref[pl.ds(pl.multiple_of(column * rows, rows), rows), tile * 128 : (tile + 1) * 128] = mixed.astype(BF)
        return carry

    lax.fori_loop(0, group, one_column, 0, unroll=2)

    hidden = jnp.concatenate(
        [part[column] for column in range(group) for part in hiddens], axis=0
    )
    hidden = hidden + dot(mixed_ref[...], col_out_ref[...])
    inner = silu(dot(norm_round(hidden, gain_ref[...]), mlp_in_ref[...])).astype(BF)
    block_out = hidden + dot(inner, mlp_out_ref[...])
    coarse = dot(block_out.astype(BF), project_ref[...]).astype(BF).astype(F32)
    for column in range(group):
        here = slice(column * rows, (column + 1) * rows)
        thin_ref[pl.ds(column, rows, stride=group), :] = coarse[here]
        for tile in range(tiles):
            wide_ref[tile, pl.ds(column, rows, stride=group), :] = block_out[here, tile * 128 : (tile + 1) * 128]
    coarse_ref[...] = thin_ref[...].reshape(coarse_ref.shape)
    for tile in range(tiles):
        block_ref[:, :, tile * 128 : (tile + 1) * 128] = wide_ref[tile].reshape(rows, group, 128)


def col_stage(queries, hiddens, pairs, bias, col_out, gain, mlp_in, mlp_out, project):
    group = 8
    chunks = len(queries)
    cols, part_rows, width = queries[0].shape
    rows = part_rows * chunks
    thin = project.shape[1]

    def by_column(array):
        return pl.BlockSpec((group,) + array.shape[1:], lambda i: (i, 0, 0))

    def whole(array):
        return pl.BlockSpec(array.shape, lambda i: (0, 0), pipeline_mode=pl.Buffered(1))

    fixed = (bias, col_out, gain, mlp_in, mlp_out, project)
    return pl.pallas_call(
        functools.partial(col_kernel, chunks, len(pairs)),
        grid=(cols // group,),
        out_shape=(
            jax.ShapeDtypeStruct((rows, cols, width), F32),
            jax.ShapeDtypeStruct((rows, cols, thin), F32),
        ),
        in_specs=[by_column(array) for array in (*queries, *hiddens, *pairs)]
        + [whole(array) for array in fixed],
        out_specs=(
            pl.BlockSpec((rows, group, width), lambda i: (0, i, 0)),
            pl.BlockSpec((rows, group, thin), lambda i: (0, i, 0)),
        ),
        scratch_shapes=[
            pltpu.VMEM((width // 128, rows * group, 128), F32),
            pltpu.VMEM((rows * group, thin), F32),
            pltpu.VMEM((rows * group, width), BF),
        ],
        compiler_params=PARAMS,
        name="col_stage",
    )(*queries, *hiddens, *pairs, *fixed)


def conv_kernel(
    flags_ref,
    coarse_ref,
    above_ref,
    below_ref,
    left_ref,
    right_ref,
    first_ref,
    second_ref,
    image_ref,
    grid_ref,
    even_ref,
    odd_ref,
    shift_ref,
):
    rows, cols, thin = coarse_ref.shape
    step = image_ref.shape[0] // 2
    index = pl.program_id(0)
    pad = grid_ref.shape[1]
    fine = even_ref.shape[1]

    def first_conv(values, low_side, right):
        return dot(values, first_ref[low_side, :, right * thin : (right + 1) * thin])

    @pl.when(index == 0)
    def _():
        grid_ref[1 : rows + 1, 8 : cols + 8, :] = coarse_ref[...]
        grid_ref[0, 8 : cols + 8, :] = above_ref[...]
        grid_ref[rows + 1, 8 : cols + 8, :] = below_ref[...]
        for row in range(rows + 2):
            grid_ref[row, 7:8, :] = left_ref[row : row + 1, :]
            grid_ref[row, cols + 8 : cols + 9, :] = right_ref[row : row + 1, :]

        def fill(row, carry):
            upper, lower = row, row + 1
            pieces = [
                grid_ref[source, 7 + shift : 7 + shift + cols, :].astype(BF)
                for source in (upper, lower)
                for shift in range(3)
            ]
            values = jnp.concatenate(pieces, axis=1)
            for phase in range(2):
                found = dot(values, first_ref[phase])
                found = silu(found)
                target = 2 * row + phase
                keep = jnp.where(
                    target == 0, flags_ref[0], jnp.where(target == 2 * rows + 1, flags_ref[1], 1.0)
                )
                found = found * keep
                even_ref[target, 0:cols, :] = found[:, :thin]
                odd_ref[target, 1 : cols + 1, :] = found[:, thin:]
            return carry

        lax.fori_loop(0, rows + 1, fill, 0)
        for side, source in ((0, left_ref), (1, right_ref)):
            near = 8 if side == 0 else cols + 7
            own = jnp.concatenate([grid_ref[row, near : near + 1, :] for row in range(rows + 2)], axis=0)
            other = source[...]
            none = jnp.zeros((rows + 1, thin), BF)
            for phase in range(2):
                parts = []
                for offset in range(2):
                    a = other[offset : offset + rows + 1].astype(BF)
                    b = own[offset : offset + rows + 1].astype(BF)
                    parts += [none, a, b] if side == 0 else [b, a, none]
                values = jnp.concatenate(parts, axis=1)
                found = silu(dot(values, first_ref[phase]))
                found = found[:, thin:] if side == 0 else found[:, :thin]
                found = found * flags_ref[2 + side]
                for row in range(rows + 1):
                    target = 2 * row + phase
                    value = found[row : row + 1]
                    if target == 0:
                        value = value * flags_ref[0]
                    if target == 2 * rows + 1:
                        value = value * flags_ref[1]
                    if side == 0:
                        odd_ref[target, 0:1, :] = value
                    else:
                        even_ref[target, cols : cols + 1, :] = value

    def second_conv(local, carry):
        row = index * step + local
        base = grid_ref[row + 1, 8 : cols + 8, :]
        for phase in range(2):
            pieces = []
            for shift in range(3):
                target = 2 * row + phase + shift
                pieces += [
                    odd_ref[target, 0:cols, :].astype(BF),
                    even_ref[target, 0:cols, :].astype(BF),
                    odd_ref[target, 1 : cols + 1, :].astype(BF),
                    even_ref[target, 1 : cols + 1, :].astype(BF),
                ]
            found = dot(jnp.concatenate(pieces, axis=1), second_ref[...])
            for right in range(2):
                image_ref[2 * local + phase, pl.ds(right, cols, stride=2), :] = (
                    base + found[:, right * thin : (right + 1) * thin]
                )
        return carry

    lax.fori_loop(0, step, second_conv, 0)


def conv_stage(flags, coarse, above, below, left, right, first, second):
    rows, cols, thin = coarse.shape
    steps = 4
    high = rows // steps

    def whole(array):
        zeros = (0,) * array.ndim
        return pl.BlockSpec(array.shape, lambda i: zeros, pipeline_mode=pl.Buffered(1))

    arrays = (coarse, above, below, left, right, first, second)
    return pl.pallas_call(
        conv_kernel,
        grid=(steps,),
        out_shape=jax.ShapeDtypeStruct((2 * rows, 2 * cols, thin), F32),
        in_specs=[SM] + [whole(array) for array in arrays],
        out_specs=pl.BlockSpec((2 * high, 2 * cols, thin), lambda i: (i, 0, 0)),
        scratch_shapes=[
            pltpu.VMEM((rows + 2, cols + 16, thin), F32),
            pltpu.VMEM((2 * rows + 2, cols + 8, thin), F32),
            pltpu.VMEM((2 * rows + 2, cols + 8, thin), F32),
            pltpu.VMEM((8, 128), F32),
        ],
        compiler_params=PARAMS,
        name="conv_stage",
    )(flags, *arrays)


def first_weights(kernel):
    wide = kernel.astype(F32)
    zero = jnp.zeros_like(wide[0, 0])
    outs = []
    for down in range(2):
        taps = (wide[0], wide[1] + wide[2]) if down == 0 else (wide[0] + wide[1], wide[2])
        lines = []
        for tap in taps:
            even = (tap[0], tap[1] + tap[2], zero)
            odd = (zero, tap[0] + tap[1], tap[2])
            lines += [jnp.concatenate([e, o], axis=1) for e, o in zip(even, odd)]
        outs.append(jnp.concatenate(lines, axis=0))
    return jnp.stack([outs[1], outs[0]]).astype(BF)


def second_weights(kernel):
    zero = jnp.zeros_like(kernel[0, 0])
    lines = []
    for down in range(3):
        even = (kernel[down, 0], kernel[down, 1], kernel[down, 2], zero)
        odd = (zero, kernel[down, 0], kernel[down, 1], kernel[down, 2])
        lines += [jnp.concatenate([e, o], axis=1) for e, o in zip(even, odd)]
    return jnp.concatenate(lines, axis=0)


def per_device(
    codes,
    starts,
    embed,
    gain_one,
    row_qkv,
    row_out,
    gain_two,
    col_qkv,
    col_out,
    gain_three,
    mlp_in,
    mlp_out,
    project,
    conv_one,
    conv_two,
):
    rows, cols = codes.shape
    vocab, width = embed.shape
    row_devices = lax.axis_size("row")
    col_devices = lax.axis_size("col")
    row_index = lax.axis_index("row")
    col_index = lax.axis_index("col")

    blocks = [codes]
    for hop in range(1, col_devices):
        pairs = [(i, i + hop) for i in range(col_devices - hop)]
        blocks.insert(0, lax.ppermute(codes, "col", pairs))
    key_ids = (jnp.concatenate(blocks, axis=1) - vocab // 2).astype(F32)
    ids = (codes - vocab // 2).astype(F32).astype(BF)

    normed = norm_round(embed.astype(F32), gain_one)
    table = jnp.dot(normed, row_qkv, preferred_element_type=F32).astype(BF)
    scale = jnp.asarray((width // HEADS) ** (-0.5), BF)
    query_table = table[:, :width] * scale
    pair_table = table[:, width:].T

    key_cols = jnp.arange(col_devices * cols, dtype=jnp.int32) - (col_devices - 1) * cols
    query_cols = jnp.arange(cols, dtype=jnp.int32)
    visible = (key_cols[None, :] <= query_cols[:, None]) & (key_cols[None, :] >= -col_index * cols)
    row_bias = jnp.where(visible, 0.0, NEGATIVE).astype(F32)

    part = rows // CHUNKS
    up = [(i, i + 2) for i in range(row_devices - 2)]
    swap = [(i, i ^ 1) for i in range(row_devices)]
    queries, hiddens, pairs = [], [], []
    key_rows = []
    for chunk in range(CHUNKS):
        here = slice(chunk * part, (chunk + 1) * part)
        own = ids[here]
        hidden, query, pair = row_stage(
            row_bias,
            key_ids[here],
            jnp.broadcast_to(own.reshape(-1, 1), (part * cols, 128)),
            jnp.broadcast_to(own.T.reshape(-1, 1), (part * cols, 128)),
            query_table,
            pair_table,
            embed,
            row_out,
            gain_two[None, :],
            col_qkv,
        )
        hiddens.append(hidden.reshape(cols, part, width))
        queries.append(query.reshape(cols, part, width))
        current = pair.reshape(cols, part, pair.shape[1])
        lines = jnp.arange(part, dtype=jnp.int32) + chunk * part
        for hop in range(row_devices // 2):
            if hop:
                current = lax.ppermute(current, "row", up)
            pairs.append(current)
            key_rows.append((row_index - 2 * hop) * rows + lines)
            pairs.append(lax.ppermute(current, "row", swap))
            key_rows.append(((row_index ^ 1) - 2 * hop) * rows + lines)
    key_rows = jnp.concatenate(key_rows)
    first_row = row_index * rows
    query_rows = first_row + jnp.arange(rows, dtype=jnp.int32)
    query_starts = lax.dynamic_slice_in_dim(starts, first_row, rows)
    visible = (key_rows[None, :] <= query_rows[:, None]) & (key_rows[None, :] >= query_starts[:, None])
    col_bias = jnp.where(visible, 0.0, NEGATIVE).astype(F32)

    block_out, coarse = col_stage(
        queries, hiddens, pairs, col_bias, col_out, gain_three[None, :], mlp_in, mlp_out, project
    )

    def along(axis, step):
        count = lax.axis_size(axis)
        return [(i, i + step) for i in range(count) if 0 <= i + step < count]

    above = lax.ppermute(coarse[rows - 1], "row", along("row", 1))
    below = lax.ppermute(coarse[0], "row", along("row", -1))

    def edge(column):
        return jnp.concatenate(
            [above[column : column + 1], coarse[:, column], below[column : column + 1]], axis=0
        )

    left = lax.ppermute(edge(cols - 1), "col", along("col", 1))
    right = lax.ppermute(edge(0), "col", along("col", -1))
    flags = jnp.stack(
        [row_index > 0, row_index < row_devices - 1, col_index > 0, col_index < col_devices - 1]
    ).astype(F32)
    image = conv_stage(
        flags, coarse, above, below, left, right, first_weights(conv_one), second_weights(conv_two)
    )
    return (block_out, image)


def solution(mesh):
    in_specs = (P("row", "col"),) + (P(),) * 14
    out_specs = (P("row", "col", None), P("row", "col", None))
    return jax.shard_map(
        per_device, mesh=mesh, in_specs=in_specs, out_specs=out_specs, check_vma=False
    )
```

```python
import functools
import jax
import jax.numpy as jnp
from jax import lax
from jax.experimental import pallas as pl
from jax.experimental.pallas import tpu as pltpu
from jax.sharding import PartitionSpec as P

HEADS = 8
CHUNKS = 2
EPS = 1e-06
NEGATIVE = -1e30
BF = jnp.bfloat16
F32 = jnp.float32
VM = pl.BlockSpec(memory_space=pltpu.VMEM)
SM = pl.BlockSpec(memory_space=pltpu.SMEM)
PARAMS = pltpu.CompilerParams(vmem_limit_bytes=56 * 1024 * 1024)


def dot(left, right):
    return jnp.dot(left, right, preferred_element_type=F32)


def dot_t(left, right):
    return lax.dot_general(left, right, (((1,), (1,)), ((), ())), preferred_element_type=F32)


def norm_round(values, norm_gain):
    scale = lax.rsqrt(jnp.mean(values * values, axis=-1, keepdims=True) + EPS)
    return (values * scale * norm_gain).astype(BF)


def silu(values):
    return values / (1.0 + jnp.exp(-values))


def one_hot(ids, vocab):
    ids = jnp.concatenate([ids] * (vocab // ids.shape[1]), axis=1)
    spots = lax.broadcasted_iota(jnp.int32, ids.shape, 1)
    spots = (spots - vocab // 2).astype(F32).astype(BF)
    return jnp.where(ids == spots, jnp.ones_like(ids), jnp.zeros_like(ids))


def low_half(shape):
    return lax.broadcasted_iota(jnp.int32, shape, len(shape) - 1) % 128 < 64


def table_kernel(embed_ref, gain_ref, row_qkv_ref, query_ref, pair_ref):
    width = embed_ref.shape[1]
    normed = norm_round(embed_ref[...].astype(F32), gain_ref[...])
    scale = jnp.asarray((width // HEADS) ** (-0.5), BF)
    query_ref[...] = dot(normed, row_qkv_ref[:, :width]).astype(BF) * scale
    for part in range(2):
        found = dot(normed, row_qkv_ref[:, (part + 1) * width : (part + 2) * width])
        pair_ref[part * width : (part + 1) * width, :] = found.T.astype(BF)


def table_stage(embed, gain, row_qkv):
    vocab, width = embed.shape
    return pl.pallas_call(
        table_kernel,
        out_shape=(
            jax.ShapeDtypeStruct((vocab, width), BF),
            jax.ShapeDtypeStruct((2 * width, vocab), BF),
        ),
        in_specs=[VM] * 3,
        out_specs=(VM, VM),
        compiler_params=PARAMS,
        name="table_stage",
    )(embed, gain, row_qkv)


def row_kernel(first, rows, split, block_count, *refs):
    place_ref = refs[0]
    blocks = refs[1 : 1 + block_count]
    (
        query_table_ref,
        pair_table_ref,
        embed_ref,
        row_out_ref,
        gain_ref,
        col_qkv_ref,
        hidden_ref,
        query_ref,
        *targets,
        mixed_ref,
        queries_ref,
        chosen_ref,
        bias_ref,
        pairs_a,
        pairs_b,
        pairs_c,
        raised_a,
        raised_b,
        raised_c,
    ) = refs[1 + block_count :]
    pair_refs = (pairs_a, pairs_b, pairs_c)
    raised_refs = (raised_a, raised_b, raised_c)
    vocab, width = query_table_ref.shape
    cols = blocks[0].shape[1]
    keys = cols * block_count
    tiles = width // 128
    half = vocab // 2

    own = (blocks[-1][first : first + rows, :] - half).astype(F32)
    lines = lax.broadcasted_iota(jnp.int32, (cols, cols), 0)
    lanes = lax.broadcasted_iota(jnp.int32, (cols, cols), 1)
    identity = jnp.where(lines == lanes, 1.0, 0.0).astype(BF)
    turned = dot_t(identity, own.astype(BF))
    for row in range(rows):
        ids = jnp.broadcast_to(turned[:, row : row + 1], (cols, 128)).astype(BF)
        chosen_ref[row * cols : (row + 1) * cols, :] = one_hot(ids, vocab)
    queries_ref[...] = dot(chosen_ref[...], query_table_ref[...]).astype(BF)
    for column in range(cols):
        ids = jnp.broadcast_to(own[:, column : column + 1], (rows, 128)).astype(BF)
        chosen_ref[column * rows : (column + 1) * rows, :] = one_hot(ids, vocab)
    line = lax.broadcasted_iota(jnp.int32, (cols, keys), 0)
    key = lax.broadcasted_iota(jnp.int32, (cols, keys), 1) - (block_count - 1) * cols
    visible = (key <= line) & (key >= -place_ref[0] * cols)
    bias = jnp.where(visible, 0.0, NEGATIVE)
    bias_ref[0:cols, :] = bias
    bias_ref[cols : 2 * cols, :] = bias

    spots = (lax.broadcasted_iota(jnp.int32, (vocab, keys), 0) - half).astype(F32).astype(BF)
    low = low_half((cols, 128))
    ones = jnp.ones((128, keys), BF)

    def gather(row, into):
        row = jnp.minimum(row, rows - 1) + first
        ids = jnp.concatenate([block[pl.ds(row, 1), :] for block in blocks], axis=1)
        ids = (ids - half).astype(F32).astype(BF)
        ids = jnp.broadcast_to(ids, (vocab, keys))
        chosen = jnp.where(ids == spots, jnp.ones_like(ids), jnp.zeros_like(ids))
        into[...] = dot(pair_table_ref[...], chosen).astype(BF)

    def score(row, source, into):
        row = jnp.clip(row, 0, rows - 1)
        for tile in range(tiles):
            here = slice(tile * 128, (tile + 1) * 128)
            query = queries_ref[pl.ds(pl.multiple_of(row * cols, cols), cols), here]
            none = jnp.zeros_like(query)
            query = jnp.concatenate([jnp.where(low, query, none), jnp.where(low, none, query)], axis=0)
            scores = dot(query, source[here, :]) + bias_ref[...]
            into[here, :] = jnp.exp(scores - jnp.max(scores, axis=1, keepdims=True)).astype(BF)

    def mix(row, source, values):
        row = jnp.maximum(row, 0)
        for tile in range(tiles):
            here = slice(tile * 128, (tile + 1) * 128)
            value = values[width + tile * 128 : width + (tile + 1) * 128, :]
            found = dot_t(source[here, :], jnp.concatenate([value, ones], axis=0))
            top = jnp.where(low, found[:cols, :128], found[cols:, :128])
            total = jnp.where(low, found[:cols, 128:], found[cols:, 128:])
            mixed_ref[tile, pl.ds(row, cols, stride=rows), :] = top / total

    def steps(turn, carry):
        for slot in range(3):
            row = 3 * turn + slot
            gather(row, pair_refs[slot])
            score(row - 1, pair_refs[(slot - 1) % 3], raised_refs[slot])
            mix(row - 2, raised_refs[(slot - 1) % 3], pair_refs[(slot - 2) % 3])
        return carry

    lax.fori_loop(0, pl.cdiv(rows + 2, 3), steps, 0)

    step = rows * cols // 2
    for block in range(2):
        here = slice(block * step, (block + 1) * step)
        mixed = [mixed_ref[tile, here, :].astype(BF) for tile in range(tiles)]
        hidden = dot(
            jnp.concatenate([chosen_ref[here, :]] + mixed, axis=1),
            jnp.concatenate([embed_ref[...], row_out_ref[...]], axis=0),
        )
        hidden_ref[here, :] = hidden
        projected = dot(norm_round(hidden, gain_ref[...]), col_qkv_ref[...]).astype(BF)
        query_ref[here, :] = projected[:, :width] * jnp.asarray((width // HEADS) ** (-0.5), BF)
        pair = projected[:, width:]
        if split:
            near, far = pair[: step // 2], pair[step // 2 :]
            outer, inner = (near, far) if block == 0 else (far, near)
            spot = slice(block * (step // 2), (block + 1) * (step // 2))
            targets[0][spot, :] = outer
            targets[1][spot, :] = inner
        else:
            targets[0][here, :] = pair


def row_stage(first, rows, split, place, blocks, query_table, pair_table, embed, row_out, gain, col_qkv):
    cols = blocks[0].shape[1]
    keys = cols * len(blocks)
    cells = rows * cols
    vocab, width = embed.shape
    return pl.pallas_call(
        functools.partial(row_kernel, first, rows, split, len(blocks)),
        out_shape=(
            jax.ShapeDtypeStruct((cells, width), F32),
            jax.ShapeDtypeStruct((cells, width), BF),
        )
        + (jax.ShapeDtypeStruct((cells // (1 + split), col_qkv.shape[1] - width), BF),) * (1 + split),
        in_specs=[SM] + [VM] * (len(blocks) + 6),
        out_specs=(VM,) * (3 + split),
        scratch_shapes=[
            pltpu.VMEM((width // 128, cells, 128), F32),
            pltpu.VMEM((cells, width), BF),
            pltpu.VMEM((cells, vocab), BF),
            pltpu.VMEM((2 * cols, keys), F32),
        ]
        + [pltpu.VMEM((2 * width, keys), BF)] * 3
        + [pltpu.VMEM((width, keys), BF)] * 3,
        compiler_params=PARAMS,
        name="row_stage",
    )(place, *blocks, query_table, pair_table, embed, row_out, gain, col_qkv)


def col_kernel(chunks, hops, edges, alias, *refs):
    blocks = 2 * hops * chunks
    queries = refs[:chunks]
    hiddens = refs[chunks : 2 * chunks]
    pairs = refs[2 * chunks : 2 * chunks + blocks]
    (
        place_ref,
        starts_ref,
        col_out_ref,
        gain_ref,
        mlp_in_ref,
        mlp_out_ref,
        project_ref,
        *rest,
    ) = refs[2 * chunks + blocks :]
    rest = rest[4:] if alias else rest
    block_ref, coarse_ref, top_ref, bottom_ref = rest[:4]
    sides = rest[4:6] if edges else None
    (
        wide_ref,
        thin_ref,
        mixed_ref,
        bias_ref,
        raised_ref,
        hidden_ref,
        normed_ref,
        inner_ref,
    ) = rest[6 if edges else 4 :]
    group, part, width = queries[0].shape
    rows = part * chunks
    tiles = width // 128
    keys = part * blocks
    index = pl.program_id(0)
    low = low_half((rows, 128))
    low_keys = low_half((keys, 128))

    @pl.when(index == 0)
    def _():
        place = place_ref[0]
        lane = lax.broadcasted_iota(jnp.int32, (8, keys), 1)
        spot = lane
        for chunk in range(chunks):
            for hop in range(hops):
                for other in range(2):
                    device = (place if other == 0 else place + 1 - 2 * (place % 2)) - 2 * hop
                    block = (chunk * hops + hop) * 2 + other
                    shift = device * rows + (chunk - block) * part
                    spot = jnp.where(lane // part == block, lane + shift, spot)
        for row in range(rows):
            query_row = place * rows + row
            start = starts_ref[query_row]
            visible = (spot >= start) & (spot <= query_row)
            bias_ref[row : row + 1, :] = jnp.where(visible, 0.0, NEGATIVE)[:1]

    def raise_scores(column):
        query = jnp.concatenate([piece[column] for piece in queries], axis=0)
        none = jnp.zeros((rows, 128), BF)
        evens, odds = [], []
        for tile in range(tiles):
            piece = query[:, tile * 128 : (tile + 1) * 128]
            evens.append(jnp.where(low, piece, none))
            odds.append(jnp.where(low, none, piece))
        pair = jnp.concatenate([piece[column] for piece in pairs], axis=0)
        turned = jnp.concatenate([pair[:, 64:], pair[:, :64]], axis=1)
        bias = jnp.concatenate([bias_ref[...]] * tiles, axis=0)
        for side, (pieces, key) in enumerate(((evens, pair), (odds, turned))):
            scores = dot_t(jnp.concatenate(pieces, axis=0), key) + bias
            raised = jnp.exp(scores - jnp.max(scores, axis=1, keepdims=True))
            raised_ref[column % 2, side] = raised.astype(BF)

    def mix(column):
        pair = jnp.concatenate([piece[column] for piece in pairs], axis=0)
        turned = jnp.concatenate([pair[:, 64:], pair[:, :64]], axis=1)
        ones = jnp.ones((keys, 128), BF)
        values = (jnp.where(low_keys, turned, ones), jnp.where(low_keys, ones, pair))
        founds = [dot(raised_ref[column % 2, side], value) for side, value in enumerate(values)]
        for tile in range(tiles):
            here = slice(tile * rows, (tile + 1) * rows)
            even, odd = founds[0][here], founds[1][here]
            total = pltpu.roll(jnp.where(low, odd, even), 64, 1)
            mixed = jnp.where(low, even, odd) / total
            mixed_ref[column * rows : (column + 1) * rows, tile * 128 : (tile + 1) * 128] = mixed.astype(BF)

    def begin():
        hidden = jnp.concatenate(
            [piece[column] for column in range(group) for piece in hiddens], axis=0
        )
        hidden = hidden + dot(mixed_ref[...], col_out_ref[...])
        hidden_ref[...] = hidden
        normed_ref[...] = norm_round(hidden, gain_ref[...])

    inner_parts = mlp_in_ref.shape[1] // 4

    def feed_in(piece):
        here = slice(piece * inner_parts, (piece + 1) * inner_parts)
        inner_ref[:, here] = silu(dot(normed_ref[...], mlp_in_ref[:, here])).astype(BF)

    def feed_out(piece):
        half = width // 2
        here = slice(piece * half, (piece + 1) * half)
        block_out = hidden_ref[:, here] + dot(inner_ref[...], mlp_out_ref[:, here])
        normed_ref[:, here] = block_out.astype(BF)
        for column in range(group):
            lines = slice(column * rows, (column + 1) * rows)
            for tile in range(half // 128):
                wide_ref[piece * (half // 128) + tile, pl.ds(column, rows, stride=group), :] = (
                    block_out[lines, tile * 128 : (tile + 1) * 128]
                )

    def finish():
        coarse = dot(normed_ref[...], project_ref[...]).astype(BF).astype(F32)
        for column in range(group):
            thin_ref[pl.ds(column, rows, stride=group), :] = coarse[column * rows : (column + 1) * rows]
        if edges:
            sides[0][0] = coarse[:rows]
            sides[1][0] = coarse[(group - 1) * rows :]
        coarse_ref[...] = thin_ref[...].reshape(coarse_ref.shape)
        top_ref[...] = thin_ref[0:group, :]
        bottom_ref[...] = thin_ref[(rows - 1) * group : rows * group, :]
        for tile in range(tiles):
            block_ref[:, :, tile * 128 : (tile + 1) * 128] = wide_ref[tile].reshape(rows, group, 128)

    feed = [functools.partial(feed_in, piece) for piece in range(4)]
    feed += [functools.partial(feed_out, piece) for piece in range(2)]
    feed += [finish]
    last = pl.num_programs(0) - 1

    def attend(between):
        raise_scores(0)
        for column in range(group):
            if column + 1 < group:
                raise_scores(column + 1)
            if column < len(between):
                between[column]()
            mix(column)

    @pl.when(index == 0)
    def _():
        attend([])

    @pl.when((index > 0) & (index < last))
    def _():
        begin()
        attend(feed)

    @pl.when(index == last)
    def _():
        begin()
        for piece in feed:
            piece()


def col_stage(queries, hiddens, pairs, whole_pairs, places, count, edges, previous, place, starts, *fixed):
    group = 8
    chunks = len(queries)
    hops = len(pairs) // (2 * chunks)
    cols, part_rows, width = queries[0].shape
    rows = part_rows * chunks
    keys = part_rows * len(pairs)
    thin = fixed[-1].shape[1]

    def now(i):
        return jnp.minimum(i, count - 1)

    def late(i):
        return jnp.maximum(i - 1, 0)

    def by_column(array, which):
        return pl.BlockSpec((group,) + array.shape[1:], lambda i: (which(i), 0, 0))

    def whole(array):
        return pl.BlockSpec(array.shape, lambda i: (0, 0), pipeline_mode=pl.Buffered(1))

    placed_now = lambda i: places(now(i))
    placed_late = lambda i: places(late(i))
    pair_specs = [
        by_column(array, placed_now if spread else now) for array, spread in zip(pairs, whole_pairs)
    ]
    out_shape = [
        jax.ShapeDtypeStruct((rows, cols, width), F32),
        jax.ShapeDtypeStruct((rows, cols, thin), F32),
        jax.ShapeDtypeStruct((cols, thin), F32),
        jax.ShapeDtypeStruct((cols, thin), F32),
    ]
    out_specs = [
        pl.BlockSpec((rows, group, width), lambda i: (0, placed_late(i), 0)),
        pl.BlockSpec((rows, group, thin), lambda i: (0, placed_late(i), 0)),
        pl.BlockSpec((group, thin), lambda i: (placed_late(i), 0)),
        pl.BlockSpec((group, thin), lambda i: (placed_late(i), 0)),
    ]
    if edges:
        out_shape += [jax.ShapeDtypeStruct((count, rows, thin), F32)] * 2
        out_specs += [pl.BlockSpec((1, rows, thin), lambda i: (late(i), 0, 0))] * 2
    first = len(queries) * 2 + len(pairs) + 2 + len(fixed)
    return pl.pallas_call(
        functools.partial(col_kernel, chunks, hops, edges, bool(previous)),
        grid=(count + 1,),
        out_shape=tuple(out_shape),
        in_specs=[by_column(array, placed_now) for array in queries]
        + [by_column(array, placed_late) for array in hiddens]
        + pair_specs
        + [SM, SM]
        + [whole(array) for array in fixed]
        + [pl.BlockSpec(memory_space=pl.ANY)] * len(previous),
        out_specs=tuple(out_specs),
        scratch_shapes=[
            pltpu.VMEM((width // 128, rows * group, 128), F32),
            pltpu.VMEM((rows * group, thin), F32),
            pltpu.VMEM((rows * group, width), BF),
            pltpu.VMEM((rows, keys), F32),
            pltpu.VMEM((2, 2, rows * (width // 128), keys), BF),
            pltpu.VMEM((rows * group, width), F32),
            pltpu.VMEM((rows * group, width), BF),
            pltpu.VMEM((rows * group, fixed[2].shape[1]), BF),
        ],
        input_output_aliases={first + i: i for i in range(len(previous))},
        compiler_params=PARAMS,
        name="col_stage",
    )(*queries, *hiddens, *pairs, place, starts, *fixed, *previous)


def weights_kernel(one_ref, two_ref, first_ref, second_ref):
    thin = one_ref.shape[2]
    none = jnp.zeros((thin, thin), BF)

    def tap(down, right):
        return one_ref[down, right].astype(F32)

    for phase in range(2):
        sums = (((0, 1), (2,)), ((0,), (1, 2)))[phase]
        for low_side in range(2):
            line = [sum(tap(down, right) for down in sums[low_side]) for right in range(3)]
            even = (line[0], line[1] + line[2], None)
            odd = (None, line[0] + line[1], line[2])
            for column in range(3):
                place = (3 * low_side + column) * thin
                for side, value in enumerate((even[column], odd[column])):
                    lane = (2 * phase + side) * thin
                    value = none if value is None else value.astype(BF)
                    first_ref[place : place + thin, lane : lane + thin] = value
    for down in range(3):
        for column in range(4):
            place = column * thin
            even = two_ref[down, column] if column < 3 else none
            odd = two_ref[down, column - 1] if column > 0 else none
            second_ref[down, place : place + thin, 0:thin] = even
            second_ref[down, place : place + thin, thin : 2 * thin] = odd


def weights_stage(one, two):
    thin = one.shape[2]
    return pl.pallas_call(
        weights_kernel,
        out_shape=(
            jax.ShapeDtypeStruct((6 * thin, 4 * thin), BF),
            jax.ShapeDtypeStruct((3, 4 * thin, 2 * thin), BF),
        ),
        in_specs=[VM, VM],
        out_specs=(VM, VM),
        compiler_params=PARAMS,
        name="weights_stage",
    )(one, two)


def conv_kernel(
    flags_ref,
    coarse_ref,
    above_ref,
    below_ref,
    left_ref,
    right_ref,
    own_left_ref,
    own_right_ref,
    first_ref,
    second_ref,
    image_ref,
    near_ref,
    fine_ref,
    edge_ref,
    wide_ref,
):
    rows, cols, thin = coarse_ref.shape
    lines = image_ref.shape[0]
    index = pl.program_id(0)
    batch = max(n for n in range(1, 12) if (rows + 1) % n == 0)
    spot = lax.broadcasted_iota(jnp.int32, (cols, thin), 0)

    @pl.when(index == 0)
    def _():
        for side, (source, cell) in enumerate(
            ((left_ref, 0), (right_ref, cols + 1), (own_left_ref, 1), (own_right_ref, cols))
        ):
            wide_ref[side, 0:1, :] = above_ref[cell : cell + 1, :]
            wide_ref[side, 1 : rows + 1, :] = source[...]
            wide_ref[side, rows + 1 : rows + 2, :] = below_ref[cell : cell + 1, :]

        def put(row, line):
            before = jnp.where(spot == 0, wide_ref[0, pl.ds(row, 1), :], pltpu.roll(line, 1, 0))
            after = jnp.where(spot == cols - 1, wide_ref[1, pl.ds(row, 1), :], pltpu.roll(line, cols - 1, 0))
            near_ref[row] = jnp.concatenate([before.astype(BF), line.astype(BF), after.astype(BF)], axis=1)

        put(0, above_ref[1 : cols + 1, :])
        put(rows + 1, below_ref[1 : cols + 1, :])

        def lay(row, carry):
            put(row + 1, coarse_ref[row])
            return carry

        lax.fori_loop(0, rows, lay, 0, unroll=4)

        none = jnp.zeros((rows + 1, thin), BF)
        for side in range(2):
            pieces = []
            for offset in range(2):
                here = slice(offset, offset + rows + 1)
                own = wide_ref[2 + side, here, :].astype(BF)
                other = wide_ref[side, here, :].astype(BF)
                pieces += [none, other, own] if side == 0 else [own, other, none]
            found = silu(dot(jnp.concatenate(pieces, axis=1), first_ref[...])) * flags_ref[2 + side]
            for phase in range(2):
                lane = (2 * phase + 1 - side) * thin
                edge_ref[side, phase, 0 : rows + 1, :] = found[:, lane : lane + thin]

        def fill(turn, carry):
            start = turn * batch
            upper = near_ref[pl.ds(start, batch)].reshape(batch * cols, 3 * thin)
            lower = near_ref[pl.ds(start + 1, batch)].reshape(batch * cols, 3 * thin)
            for phase in range(2):
                lanes = slice(2 * phase * thin, 2 * (phase + 1) * thin)
                found = silu(
                    dot(upper, first_ref[: 3 * thin, lanes]) + dot(lower, first_ref[3 * thin :, lanes])
                )
                for row in range(batch):
                    even = found[row * cols : (row + 1) * cols, :thin]
                    odd = found[row * cols : (row + 1) * cols, thin:]
                    edges = [edge_ref[side, phase, pl.ds(start + row, 1), :] for side in range(2)]
                    before = jnp.where(spot == 0, edges[0], pltpu.roll(odd, 1, 0))
                    after = jnp.where(spot == cols - 1, edges[1], pltpu.roll(even, cols - 1, 0))
                    fine_ref[2 * (start + row) + phase] = jnp.concatenate(
                        [before.astype(BF), even.astype(BF), odd.astype(BF), after.astype(BF)], axis=1
                    )
            return carry

        lax.fori_loop(0, (rows + 1) // batch, fill, 0)
        for side, line in ((0, 0), (1, 2 * rows + 1)):
            fine_ref[line] = (fine_ref[line].astype(F32) * flags_ref[side]).astype(BF)

    step = 8

    def second_conv(turn, carry):
        start = index * lines + turn * step
        found = jnp.zeros((step * cols, 2 * thin), F32)
        for shift in range(3):
            values = fine_ref[pl.ds(start + shift, step)].reshape(step * cols, 4 * thin)
            found = found + dot(values, second_ref[shift])
        for line in range(step):
            base = coarse_ref[start // 2 + line // 2]
            for right in range(2):
                image_ref[turn * step + line, pl.ds(right, cols, stride=2), :] = (
                    base + found[line * cols : (line + 1) * cols, right * thin : (right + 1) * thin]
                )
        return carry

    lax.fori_loop(0, lines // step, second_conv, 0)


def conv_stage(flags, *arrays):
    rows, cols, thin = arrays[0].shape
    steps = 4
    lines = 2 * rows // steps

    def whole(array):
        zeros = (0,) * array.ndim
        return pl.BlockSpec(array.shape, lambda i: zeros, pipeline_mode=pl.Buffered(1))

    return pl.pallas_call(
        conv_kernel,
        grid=(steps,),
        out_shape=jax.ShapeDtypeStruct((2 * rows, 2 * cols, thin), F32),
        in_specs=[SM] + [whole(array) for array in arrays],
        out_specs=pl.BlockSpec((lines, 2 * cols, thin), lambda i: (i, 0, 0)),
        scratch_shapes=[
            pltpu.VMEM((rows + 2, cols, 3 * thin), BF),
            pltpu.VMEM((2 * rows + 2, cols, 4 * thin), BF),
            pltpu.VMEM((2, 2, rows + 8, thin), F32),
            pltpu.VMEM((4, rows + 8, thin), F32),
        ],
        compiler_params=PARAMS,
        name="conv_stage",
    )(flags, *arrays)


def per_device(
    codes,
    starts,
    embed,
    gain_one,
    row_qkv,
    row_out,
    gain_two,
    col_qkv,
    col_out,
    gain_three,
    mlp_in,
    mlp_out,
    project,
    conv_one,
    conv_two,
):
    rows, cols = codes.shape
    _, width = embed.shape
    row_devices = lax.axis_size("row")
    col_devices = lax.axis_size("col")
    row_index = lax.axis_index("row")
    col_index = lax.axis_index("col")

    blocks = [codes]
    for hop in range(1, col_devices):
        ahead = [(i, i + hop) for i in range(col_devices - hop)]
        blocks.insert(0, lax.ppermute(codes, "col", ahead))
    query_table, pair_table = table_stage(embed, gain_one[None, :], row_qkv)
    first_weights, second_weights = weights_stage(conv_one, conv_two)

    part = rows // CHUNKS
    hops = row_devices // 2

    def ahead(step):
        return [(i, i + step) for i in range(row_devices - step)]

    def spread(block, direct):
        held = [block]
        for hop in range(1, hops):
            if hop <= 2 or (direct and hop == 3):
                held.append(lax.ppermute(block, "row", ahead(2 * hop)))
            else:
                held.append(lax.ppermute(held[-1], "row", ahead(2)))
        swap = [(i, i ^ 1) for i in range(row_devices)]
        every = []
        for block in held:
            every += [block, lax.ppermute(block, "row", swap)]
        return every

    queries, hiddens, pairs = [], [], []
    for chunk in range(CHUNKS):
        split = chunk == CHUNKS - 1
        hidden, query, *pair = row_stage(
            chunk * part,
            part,
            split,
            col_index[None],
            blocks,
            query_table,
            pair_table,
            embed,
            row_out,
            gain_two[None, :],
            col_qkv,
        )
        hiddens.append(hidden.reshape(cols, part, width))
        queries.append(query.reshape(cols, part, width))
        for block in pair:
            block = block.reshape(cols // (1 + split), part, block.shape[1])
            pairs.append(spread(block, split))

    count = cols // 16
    fixed = (row_index[None], starts, col_out, gain_three[None, :], mlp_in, mlp_out, project)
    firm = sum(pairs[:-2], [])
    spread_out = (True,) * len(firm) + (False,) * len(pairs[-1])
    block_out, coarse, top, bottom, first_cols, last_cols = col_stage(
        queries,
        hiddens,
        firm + pairs[-2],
        spread_out,
        lambda i: i + jnp.where(i < count // 2, 0, count),
        count,
        True,
        (),
        *fixed,
    )
    first_col, last_col = first_cols[0], last_cols[count - 1]

    def along(axis, step):
        size = lax.axis_size(axis)
        return [(i, i + step) for i in range(size) if 0 <= i + step < size]

    left = lax.ppermute(last_col, "col", along("col", 1))
    right = lax.ppermute(first_col, "col", along("col", -1))
    block_out, coarse, top, bottom = col_stage(
        queries,
        hiddens,
        firm + pairs[-1],
        spread_out,
        lambda i: i + count // 2,
        count,
        False,
        (block_out, coarse, top, bottom),
        *fixed,
    )

    def wide(line, row):
        return jnp.concatenate([left[row : row + 1], line, right[row : row + 1]], axis=0)

    above = lax.ppermute(wide(bottom, rows - 1), "row", along("row", 1))
    below = lax.ppermute(wide(top, 0), "row", along("row", -1))
    flags = jnp.stack(
        [row_index > 0, row_index < row_devices - 1, col_index > 0, col_index < col_devices - 1]
    ).astype(F32)
    image = conv_stage(
        flags,
        coarse,
        above,
        below,
        left,
        right,
        first_col,
        last_col,
        first_weights,
        second_weights,
    )
    return (block_out, image)


def solution(mesh):
    in_specs = (P("row", "col"),) + (P(),) * 14
    out_specs = (P("row", "col", None), P("row", "col", None))
    return jax.shard_map(
        per_device, mesh=mesh, in_specs=in_specs, out_specs=out_specs, check_vma=False
    )
```

```python
import functools
import jax
import jax.numpy as jnp
from jax import lax
from jax.experimental import pallas as pl
from jax.experimental.pallas import tpu as pltpu
from jax.sharding import PartitionSpec as P

HEADS = 8
CHUNKS = 2
EPS = 1e-06
NEGATIVE = -1e30
BF = jnp.bfloat16
F32 = jnp.float32
VM = pl.BlockSpec(memory_space=pltpu.VMEM)
SM = pl.BlockSpec(memory_space=pltpu.SMEM)
PARAMS = pltpu.CompilerParams(vmem_limit_bytes=56 * 1024 * 1024)


def dot(left, right):
    return jnp.dot(left, right, preferred_element_type=F32)


def dot_t(left, right):
    return lax.dot_general(left, right, (((1,), (1,)), ((), ())), preferred_element_type=F32)


def norm_round(values, norm_gain):
    scale = lax.rsqrt(jnp.mean(values * values, axis=-1, keepdims=True) + EPS)
    return (values * scale * norm_gain).astype(BF)


def silu(values):
    return values / (1.0 + jnp.exp(-values))


def one_hot(ids, vocab):
    ids = jnp.concatenate([ids] * (vocab // ids.shape[1]), axis=1)
    spots = lax.broadcasted_iota(jnp.int32, ids.shape, 1)
    spots = (spots - vocab // 2).astype(F32).astype(BF)
    return jnp.where(ids == spots, jnp.ones_like(ids), jnp.zeros_like(ids))


def low_half(shape):
    return lax.broadcasted_iota(jnp.int32, shape, len(shape) - 1) % 128 < 64


def table_kernel(embed_ref, gain_ref, row_qkv_ref, query_ref, pair_ref):
    width = embed_ref.shape[1]
    normed = norm_round(embed_ref[...].astype(F32), gain_ref[...])
    scale = jnp.asarray((width // HEADS) ** (-0.5), BF)
    query_ref[...] = dot(normed, row_qkv_ref[:, :width]).astype(BF) * scale
    for part in range(2):
        found = dot(normed, row_qkv_ref[:, (part + 1) * width : (part + 2) * width])
        pair_ref[part * width : (part + 1) * width, :] = found.T.astype(BF)


def table_stage(embed, gain, row_qkv):
    vocab, width = embed.shape
    return pl.pallas_call(
        table_kernel,
        out_shape=(
            jax.ShapeDtypeStruct((vocab, width), BF),
            jax.ShapeDtypeStruct((2 * width, vocab), BF),
        ),
        in_specs=[VM] * 3,
        out_specs=(VM, VM),
        compiler_params=PARAMS,
        name="table_stage",
    )(embed, gain, row_qkv)


def row_kernel(first, rows, split, block_count, *refs):
    place_ref = refs[0]
    blocks = refs[1 : 1 + block_count]
    (
        query_table_ref,
        pair_table_ref,
        embed_ref,
        row_out_ref,
        gain_ref,
        col_qkv_ref,
        hidden_ref,
        query_ref,
        *targets,
        mixed_ref,
        queries_ref,
        chosen_ref,
        bias_ref,
        pairs_a,
        pairs_b,
        pairs_c,
        raised_a,
        raised_b,
        raised_c,
    ) = refs[1 + block_count :]
    pair_refs = (pairs_a, pairs_b, pairs_c)
    raised_refs = (raised_a, raised_b, raised_c)
    vocab, width = query_table_ref.shape
    cols = blocks[0].shape[1]
    keys = cols * block_count
    tiles = width // 128
    half = vocab // 2

    own = (blocks[-1][first : first + rows, :] - half).astype(F32)
    lines = lax.broadcasted_iota(jnp.int32, (cols, cols), 0)
    lanes = lax.broadcasted_iota(jnp.int32, (cols, cols), 1)
    identity = jnp.where(lines == lanes, 1.0, 0.0).astype(BF)
    turned = dot_t(identity, own.astype(BF))
    for row in range(rows):
        ids = jnp.broadcast_to(turned[:, row : row + 1], (cols, 128)).astype(BF)
        chosen_ref[row * cols : (row + 1) * cols, :] = one_hot(ids, vocab)
    queries_ref[...] = dot(chosen_ref[...], query_table_ref[...]).astype(BF)
    for column in range(cols):
        ids = jnp.broadcast_to(own[:, column : column + 1], (rows, 128)).astype(BF)
        chosen_ref[column * rows : (column + 1) * rows, :] = one_hot(ids, vocab)
    line = lax.broadcasted_iota(jnp.int32, (cols, keys), 0)
    key = lax.broadcasted_iota(jnp.int32, (cols, keys), 1) - (block_count - 1) * cols
    visible = (key <= line) & (key >= -place_ref[0] * cols)
    bias = jnp.where(visible, 0.0, NEGATIVE)
    bias_ref[0:cols, :] = bias
    bias_ref[cols : 2 * cols, :] = bias

    spots = (lax.broadcasted_iota(jnp.int32, (vocab, keys), 0) - half).astype(F32).astype(BF)
    low = low_half((cols, 128))
    ones = jnp.ones((128, keys), BF)

    def gather(row, into):
        row = jnp.minimum(row, rows - 1) + first
        ids = jnp.concatenate([block[pl.ds(row, 1), :] for block in blocks], axis=1)
        ids = (ids - half).astype(F32).astype(BF)
        ids = jnp.broadcast_to(ids, (vocab, keys))
        chosen = jnp.where(ids == spots, jnp.ones_like(ids), jnp.zeros_like(ids))
        into[...] = dot(pair_table_ref[...], chosen).astype(BF)

    def score(row, source, into):
        row = jnp.clip(row, 0, rows - 1)
        for tile in range(tiles):
            here = slice(tile * 128, (tile + 1) * 128)
            query = queries_ref[pl.ds(pl.multiple_of(row * cols, cols), cols), here]
            none = jnp.zeros_like(query)
            query = jnp.concatenate([jnp.where(low, query, none), jnp.where(low, none, query)], axis=0)
            scores = dot(query, source[here, :]) + bias_ref[...]
            into[here, :] = jnp.exp(scores - jnp.max(scores, axis=1, keepdims=True)).astype(BF)

    def mix(row, source, values):
        row = jnp.maximum(row, 0)
        for tile in range(tiles):
            here = slice(tile * 128, (tile + 1) * 128)
            value = values[width + tile * 128 : width + (tile + 1) * 128, :]
            found = dot_t(source[here, :], jnp.concatenate([value, ones], axis=0))
            top = jnp.where(low, found[:cols, :128], found[cols:, :128])
            total = jnp.where(low, found[:cols, 128:], found[cols:, 128:])
            mixed_ref[tile, pl.ds(row, cols, stride=rows), :] = top / total

    def steps(turn, carry):
        for slot in range(3):
            row = 3 * turn + slot
            gather(row, pair_refs[slot])
            score(row - 1, pair_refs[(slot - 1) % 3], raised_refs[slot])
            mix(row - 2, raised_refs[(slot - 1) % 3], pair_refs[(slot - 2) % 3])
        return carry

    lax.fori_loop(0, pl.cdiv(rows + 2, 3), steps, 0)

    step = rows * cols // 2
    for block in range(2):
        here = slice(block * step, (block + 1) * step)
        mixed = [mixed_ref[tile, here, :].astype(BF) for tile in range(tiles)]
        hidden = dot(
            jnp.concatenate([chosen_ref[here, :]] + mixed, axis=1),
            jnp.concatenate([embed_ref[...], row_out_ref[...]], axis=0),
        )
        hidden_ref[here, :] = hidden
        projected = dot(norm_round(hidden, gain_ref[...]), col_qkv_ref[...]).astype(BF)
        query_ref[here, :] = projected[:, :width] * jnp.asarray((width // HEADS) ** (-0.5), BF)
        pair = projected[:, width:]
        if split:
            near, far = pair[: step // 2], pair[step // 2 :]
            outer, inner = (near, far) if block == 0 else (far, near)
            spot = slice(block * (step // 2), (block + 1) * (step // 2))
            targets[0][spot, :] = outer
            targets[1][spot, :] = inner
        else:
            targets[0][here, :] = pair


def row_stage(first, rows, split, place, blocks, query_table, pair_table, embed, row_out, gain, col_qkv):
    cols = blocks[0].shape[1]
    keys = cols * len(blocks)
    cells = rows * cols
    vocab, width = embed.shape
    return pl.pallas_call(
        functools.partial(row_kernel, first, rows, split, len(blocks)),
        out_shape=(
            jax.ShapeDtypeStruct((cells, width), F32),
            jax.ShapeDtypeStruct((cells, width), BF),
        )
        + (jax.ShapeDtypeStruct((cells // (1 + split), col_qkv.shape[1] - width), BF),) * (1 + split),
        in_specs=[SM] + [VM] * (len(blocks) + 6),
        out_specs=(VM,) * (3 + split),
        scratch_shapes=[
            pltpu.VMEM((width // 128, cells, 128), F32),
            pltpu.VMEM((cells, width), BF),
            pltpu.VMEM((cells, vocab), BF),
            pltpu.VMEM((2 * cols, keys), F32),
        ]
        + [pltpu.VMEM((2 * width, keys), BF)] * 3
        + [pltpu.VMEM((width, keys), BF)] * 3,
        compiler_params=PARAMS,
        name="row_stage",
    )(place, *blocks, query_table, pair_table, embed, row_out, gain, col_qkv)


def col_kernel(chunks, hops, edges, alias, *refs):
    blocks = 2 * hops * chunks
    queries = refs[:chunks]
    hiddens = refs[chunks : 2 * chunks]
    pairs = refs[2 * chunks : 2 * chunks + blocks]
    (
        place_ref,
        starts_ref,
        col_out_ref,
        gain_ref,
        mlp_in_ref,
        mlp_out_ref,
        project_ref,
        *rest,
    ) = refs[2 * chunks + blocks :]
    rest = rest[4:] if alias else rest
    block_ref, coarse_ref, top_ref, bottom_ref = rest[:4]
    sides = rest[4:6] if edges else None
    (
        wide_ref,
        thin_ref,
        mixed_ref,
        bias_ref,
        raised_ref,
        turned_ref,
        hidden_ref,
        normed_ref,
        inner_ref,
    ) = rest[6 if edges else 4 :]
    group, part, width = queries[0].shape
    rows = part * chunks
    tiles = width // 128
    keys = part * blocks
    index = pl.program_id(0)
    low = low_half((rows, 128))
    low_keys = low_half((keys, 128))

    @pl.when(index == 0)
    def _():
        place = place_ref[0]
        lane = lax.broadcasted_iota(jnp.int32, (8, keys), 1)
        spot = lane
        for chunk in range(chunks):
            for hop in range(hops):
                for other in range(2):
                    device = (place if other == 0 else place + 1 - 2 * (place % 2)) - 2 * hop
                    block = (chunk * hops + hop) * 2 + other
                    shift = device * rows + (chunk - block) * part
                    spot = jnp.where(lane // part == block, lane + shift, spot)
        for row in range(rows):
            query_row = place * rows + row
            start = starts_ref[query_row]
            visible = (spot >= start) & (spot <= query_row)
            bias_ref[row : row + 1, :] = jnp.where(visible, 0.0, NEGATIVE)[:1]

    def raise_scores(column):
        query = jnp.concatenate([piece[column] for piece in queries], axis=0)
        none = jnp.zeros((rows, 128), BF)
        evens, odds = [], []
        for tile in range(tiles):
            piece = query[:, tile * 128 : (tile + 1) * 128]
            evens.append(jnp.where(low, piece, none))
            odds.append(jnp.where(low, none, piece))
        pair = jnp.concatenate([piece[column] for piece in pairs], axis=0)
        turned = jnp.concatenate([pair[:, 64:], pair[:, :64]], axis=1)
        turned_ref[column % 3] = turned
        bias = jnp.concatenate([bias_ref[...]] * tiles, axis=0)
        for side, (pieces, key) in enumerate(((evens, pair), (odds, turned))):
            scores = dot_t(jnp.concatenate(pieces, axis=0), key) + bias
            raised = jnp.exp(scores - jnp.max(scores, axis=1, keepdims=True))
            raised_ref[column % 3, side] = raised.astype(BF)

    def mix(column):
        pair = jnp.concatenate([piece[column] for piece in pairs], axis=0)
        turned = turned_ref[column % 3]
        ones = jnp.ones((keys, 128), BF)
        values = (jnp.where(low_keys, turned, ones), jnp.where(low_keys, ones, pair))
        founds = [dot(raised_ref[column % 3, side], value) for side, value in enumerate(values)]
        for tile in range(tiles):
            here = slice(tile * rows, (tile + 1) * rows)
            even, odd = founds[0][here], founds[1][here]
            total = pltpu.roll(jnp.where(low, odd, even), 64, 1)
            mixed = jnp.where(low, even, odd) / total
            mixed_ref[column * rows : (column + 1) * rows, tile * 128 : (tile + 1) * 128] = mixed.astype(BF)

    def begin():
        hidden = jnp.concatenate(
            [piece[column] for column in range(group) for piece in hiddens], axis=0
        )
        hidden = hidden + dot(mixed_ref[...], col_out_ref[...])
        hidden_ref[...] = hidden
        normed_ref[...] = norm_round(hidden, gain_ref[...])

    inner_parts = mlp_in_ref.shape[1] // 4

    def feed_in(piece):
        here = slice(piece * inner_parts, (piece + 1) * inner_parts)
        inner_ref[:, here] = silu(dot(normed_ref[...], mlp_in_ref[:, here])).astype(BF)

    def feed_out(piece):
        half = width // 2
        here = slice(piece * half, (piece + 1) * half)
        block_out = hidden_ref[:, here] + dot(inner_ref[...], mlp_out_ref[:, here])
        normed_ref[:, here] = block_out.astype(BF)
        for column in range(group):
            lines = slice(column * rows, (column + 1) * rows)
            for tile in range(half // 128):
                wide_ref[piece * (half // 128) + tile, pl.ds(column, rows, stride=group), :] = (
                    block_out[lines, tile * 128 : (tile + 1) * 128]
                )

    def finish():
        coarse = dot(normed_ref[...], project_ref[...]).astype(BF).astype(F32)
        for column in range(group):
            thin_ref[pl.ds(column, rows, stride=group), :] = coarse[column * rows : (column + 1) * rows]
        if edges:
            sides[0][...] = jnp.where(index == 1, coarse[:rows], sides[0][...])
            sides[1][...] = coarse[(group - 1) * rows :]
        coarse_ref[...] = thin_ref[...].reshape(coarse_ref.shape)
        top_ref[...] = thin_ref[0:group, :]
        bottom_ref[...] = thin_ref[(rows - 1) * group : rows * group, :]
        for tile in range(tiles):
            block_ref[:, :, tile * 128 : (tile + 1) * 128] = wide_ref[tile].reshape(rows, group, 128)

    feed = [functools.partial(feed_in, piece) for piece in range(4)]
    feed += [functools.partial(feed_out, piece) for piece in range(2)]
    feed += [finish]
    last = pl.num_programs(0) - 1

    def attend(between):
        for column in range(2):
            raise_scores(column)
        for column in range(group):
            if column + 2 < group:
                raise_scores(column + 2)
            if column < len(between):
                between[column]()
            mix(column)

    @pl.when(index == 0)
    def _():
        attend([])

    @pl.when((index > 0) & (index < last))
    def _():
        begin()
        attend(feed)

    @pl.when(index == last)
    def _():
        begin()
        for piece in feed:
            piece()


def col_stage(queries, hiddens, pairs, whole_pairs, places, count, edges, previous, place, starts, *fixed):
    group = 8
    chunks = len(queries)
    hops = len(pairs) // (2 * chunks)
    cols, part_rows, width = queries[0].shape
    rows = part_rows * chunks
    keys = part_rows * len(pairs)
    thin = fixed[-1].shape[1]

    def now(i):
        return jnp.minimum(i, count - 1)

    def late(i):
        return jnp.maximum(i - 1, 0)

    def by_column(array, which):
        return pl.BlockSpec((group,) + array.shape[1:], lambda i: (which(i), 0, 0))

    def whole(array):
        return pl.BlockSpec(array.shape, lambda i: (0, 0), pipeline_mode=pl.Buffered(1))

    placed_now = lambda i: places(now(i))
    placed_late = lambda i: places(late(i))
    pair_specs = [
        by_column(array, placed_now if spread else now) for array, spread in zip(pairs, whole_pairs)
    ]
    out_shape = [
        jax.ShapeDtypeStruct((rows, cols, width), F32),
        jax.ShapeDtypeStruct((rows, cols, thin), F32),
        jax.ShapeDtypeStruct((cols, thin), F32),
        jax.ShapeDtypeStruct((cols, thin), F32),
    ]
    out_specs = [
        pl.BlockSpec((rows, group, width), lambda i: (0, placed_late(i), 0)),
        pl.BlockSpec((rows, group, thin), lambda i: (0, placed_late(i), 0)),
        pl.BlockSpec((group, thin), lambda i: (placed_late(i), 0)),
        pl.BlockSpec((group, thin), lambda i: (placed_late(i), 0)),
    ]
    if edges:
        out_shape += [jax.ShapeDtypeStruct((rows, thin), F32)] * 2
        out_specs += [pl.BlockSpec((rows, thin), lambda i: (0, 0))] * 2
    first = len(queries) * 2 + len(pairs) + 2 + len(fixed)
    return pl.pallas_call(
        functools.partial(col_kernel, chunks, hops, edges, bool(previous)),
        grid=(count + 1,),
        out_shape=tuple(out_shape),
        in_specs=[by_column(array, placed_now) for array in queries]
        + [by_column(array, placed_late) for array in hiddens]
        + pair_specs
        + [SM, SM]
        + [whole(array) for array in fixed]
        + [pl.BlockSpec(memory_space=pl.ANY)] * len(previous),
        out_specs=tuple(out_specs),
        scratch_shapes=[
            pltpu.VMEM((width // 128, rows * group, 128), F32),
            pltpu.VMEM((rows * group, thin), F32),
            pltpu.VMEM((rows * group, width), BF),
            pltpu.VMEM((rows, keys), F32),
            pltpu.VMEM((3, 2, rows * (width // 128), keys), BF),
            pltpu.VMEM((3, keys, 128), BF),
            pltpu.VMEM((rows * group, width), F32),
            pltpu.VMEM((rows * group, width), BF),
            pltpu.VMEM((rows * group, fixed[2].shape[1]), BF),
        ],
        input_output_aliases={first + i: i for i in range(len(previous))},
        compiler_params=PARAMS,
        name="col_stage",
    )(*queries, *hiddens, *pairs, place, starts, *fixed, *previous)


def weights_kernel(one_ref, two_ref, first_ref, second_ref):
    thin = one_ref.shape[2]
    none = jnp.zeros((thin, thin), BF)

    def tap(down, right):
        return one_ref[down, right].astype(F32)

    for phase in range(2):
        sums = (((0, 1), (2,)), ((0,), (1, 2)))[phase]
        for low_side in range(2):
            line = [sum(tap(down, right) for down in sums[low_side]) for right in range(3)]
            even = (line[0], line[1] + line[2], None)
            odd = (None, line[0] + line[1], line[2])
            for column in range(3):
                place = (3 * low_side + column) * thin
                for side, value in enumerate((even[column], odd[column])):
                    lane = (2 * phase + side) * thin
                    value = none if value is None else value.astype(BF)
                    first_ref[place : place + thin, lane : lane + thin] = value
    for down in range(3):
        for column in range(4):
            place = column * thin
            even = two_ref[down, column] if column < 3 else none
            odd = two_ref[down, column - 1] if column > 0 else none
            second_ref[down, place : place + thin, 0:thin] = even
            second_ref[down, place : place + thin, thin : 2 * thin] = odd


def weights_stage(one, two):
    thin = one.shape[2]
    return pl.pallas_call(
        weights_kernel,
        out_shape=(
            jax.ShapeDtypeStruct((6 * thin, 4 * thin), BF),
            jax.ShapeDtypeStruct((3, 4 * thin, 2 * thin), BF),
        ),
        in_specs=[VM, VM],
        out_specs=(VM, VM),
        compiler_params=PARAMS,
        name="weights_stage",
    )(one, two)


def conv_kernel(
    place_ref,
    coarse_ref,
    left_ref,
    right_ref,
    own_left_ref,
    own_right_ref,
    first_ref,
    second_ref,
    image_ref,
    near_ref,
    fine_ref,
    edge_ref,
):
    rows, cols, thin = coarse_ref.shape
    lines = image_ref.shape[0]
    index = pl.program_id(0)
    batch = max(n for n in range(1, 12) if (rows + 1) % n == 0)
    spot = lax.broadcasted_iota(jnp.int32, (cols, thin), 0)

    @pl.when(index == 0)
    def _():
        def put(row, carry):
            line = coarse_ref[row]
            before = jnp.where(spot == 0, left_ref[pl.ds(row, 1), :], pltpu.roll(line, 1, 0))
            after = jnp.where(spot == cols - 1, right_ref[pl.ds(row, 1), :], pltpu.roll(line, cols - 1, 0))
            near_ref[row + 1] = jnp.concatenate([before.astype(BF), line.astype(BF), after.astype(BF)], axis=1)
            return carry

        near_ref[0] = jnp.zeros((cols, 3 * thin), BF)
        near_ref[rows + 1] = jnp.zeros((cols, 3 * thin), BF)
        lax.fori_loop(0, rows, put, 0, unroll=4)

        none = jnp.zeros((rows - 1, thin), BF)
        for side in range(2):
            pieces = []
            for offset in range(2):
                here = slice(offset, offset + rows - 1)
                own = (own_left_ref, own_right_ref)[side][here, :].astype(BF)
                other = (left_ref, right_ref)[side][here, :].astype(BF)
                pieces += [none, other, own] if side == 0 else [own, other, none]
            found = silu(dot(jnp.concatenate(pieces, axis=1), first_ref[...]))
            found = found * jnp.where(place_ref[2 + side] == 0, 0.0, 1.0)
            for phase in range(2):
                lane = (2 * phase + 1 - side) * thin
                edge_ref[side, phase, 1:rows, :] = found[:, lane : lane + thin]

        def fill(turn, carry):
            start = turn * batch
            upper = near_ref[pl.ds(start, batch)].reshape(batch * cols, 3 * thin)
            lower = near_ref[pl.ds(start + 1, batch)].reshape(batch * cols, 3 * thin)
            for phase in range(2):
                lanes = slice(2 * phase * thin, 2 * (phase + 1) * thin)
                found = silu(
                    dot(upper, first_ref[: 3 * thin, lanes]) + dot(lower, first_ref[3 * thin :, lanes])
                )
                for row in range(batch):
                    even = found[row * cols : (row + 1) * cols, :thin]
                    odd = found[row * cols : (row + 1) * cols, thin:]
                    edges = [edge_ref[side, phase, pl.ds(start + row, 1), :] for side in range(2)]
                    before = jnp.where(spot == 0, edges[0], pltpu.roll(odd, 1, 0))
                    after = jnp.where(spot == cols - 1, edges[1], pltpu.roll(even, cols - 1, 0))
                    fine_ref[2 * (start + row) + phase] = jnp.concatenate(
                        [before.astype(BF), even.astype(BF), odd.astype(BF), after.astype(BF)], axis=1
                    )
            return carry

        lax.fori_loop(0, (rows + 1) // batch, fill, 0)

    step = 8

    def second_conv(turn, carry):
        start = index * lines + turn * step
        found = jnp.zeros((step * cols, 2 * thin), F32)
        for shift in range(3):
            values = fine_ref[pl.ds(start + shift, step)].reshape(step * cols, 4 * thin)
            found = found + dot(values, second_ref[shift])
        for line in range(step):
            base = coarse_ref[start // 2 + line // 2]
            for right in range(2):
                image_ref[turn * step + line, pl.ds(right, cols, stride=2), :] = (
                    base + found[line * cols : (line + 1) * cols, right * thin : (right + 1) * thin]
                )
        return carry

    lax.fori_loop(0, lines // step, second_conv, 0)


def conv_stage(place, *arrays):
    rows, cols, thin = arrays[0].shape
    steps = 4
    lines = 2 * rows // steps

    def whole(array):
        zeros = (0,) * array.ndim
        return pl.BlockSpec(array.shape, lambda i: zeros, pipeline_mode=pl.Buffered(1))

    return pl.pallas_call(
        conv_kernel,
        grid=(steps,),
        out_shape=jax.ShapeDtypeStruct((2 * rows, 2 * cols, thin), F32),
        in_specs=[SM] + [whole(array) for array in arrays],
        out_specs=pl.BlockSpec((lines, 2 * cols, thin), lambda i: (i, 0, 0)),
        scratch_shapes=[
            pltpu.VMEM((rows + 2, cols, 3 * thin), BF),
            pltpu.VMEM((2 * rows + 2, cols, 4 * thin), BF),
            pltpu.VMEM((2, 2, rows + 8, thin), F32),
        ],
        compiler_params=PARAMS,
        name="conv_stage",
    )(place, *arrays)


def border_kernel(
    place_ref,
    coarse_ref,
    above_ref,
    below_ref,
    left_ref,
    right_ref,
    first_ref,
    second_ref,
    whole_ref,
    image_ref,
):
    rows = left_ref.shape[0]
    _, cols, thin = coarse_ref.shape
    index = pl.program_id(0)
    upper = index == 0
    spot = lax.broadcasted_iota(jnp.int32, (cols, thin), 0)

    def pick(one, two):
        return jnp.where(upper, one, two)

    lines = (
        pick(above_ref[1 : cols + 1, :], coarse_ref[0]),
        pick(coarse_ref[0], coarse_ref[1]),
        pick(coarse_ref[1], below_ref[1 : cols + 1, :]),
    )
    sides = []
    for source, cell in ((left_ref, 0), (right_ref, cols + 1)):
        sides.append(
            (
                pick(above_ref[cell : cell + 1, :], source[rows - 2 : rows - 1, :]),
                pick(source[0:1, :], source[rows - 1 : rows, :]),
                pick(source[1:2, :], below_ref[cell : cell + 1, :]),
            )
        )
    near = []
    for line, left, right in zip(lines, *sides):
        before = jnp.where(spot == 0, left, pltpu.roll(line, 1, 0))
        after = jnp.where(spot == cols - 1, right, pltpu.roll(line, cols - 1, 0))
        near.append(jnp.concatenate([before.astype(BF), line.astype(BF), after.astype(BF)], axis=1))
    values = jnp.concatenate(
        [jnp.concatenate([near[row], near[row + 1]], axis=1) for row in range(2)], axis=0
    )
    found = silu(dot(values, first_ref[...]))
    none = jnp.zeros((1, thin), F32)
    edge = []
    for side in range(2):
        for row in range(2):
            pieces = []
            for offset in range(2):
                own = lines[row + offset][0:1] if side == 0 else lines[row + offset][cols - 1 : cols]
                other = sides[side][row + offset]
                pieces += [none, other, own] if side == 0 else [own, other, none]
            edge.append(jnp.concatenate(pieces, axis=1))
    edge = jnp.concatenate(edge + [jnp.zeros_like(edge[0])] * 4, axis=0).astype(BF)
    edge = silu(dot(edge, first_ref[...]))
    fine = []
    for row in range(2):
        for phase in range(2):
            lane = 2 * phase * thin
            even = found[row * cols : (row + 1) * cols, lane : lane + thin]
            odd = found[row * cols : (row + 1) * cols, lane + thin : lane + 2 * thin]
            left = edge[row : row + 1, lane + thin : lane + 2 * thin]
            right = edge[2 + row : 3 + row, lane : lane + thin]
            left = left * jnp.where(place_ref[2] == 0, 0.0, 1.0)
            right = right * jnp.where(place_ref[3] == 0, 0.0, 1.0)
            before = jnp.where(spot == 0, left, pltpu.roll(odd, 1, 0))
            after = jnp.where(spot == cols - 1, right, pltpu.roll(even, cols - 1, 0))
            line = jnp.concatenate([before, even, odd, after], axis=1)
            if row == phase:
                keep = jnp.where(place_ref[row] == 0, 0.0, 1.0)
                line = line * jnp.where(upper if row == 0 else index == 1, keep, 1.0)
            fine.append(line.astype(BF))
    total = jnp.zeros((2 * cols, 2 * thin), F32)
    for shift in range(3):
        values = jnp.concatenate([fine[shift], fine[shift + 1]], axis=0)
        total = total + dot(values, second_ref[shift])
    base = pick(coarse_ref[0], coarse_ref[1])
    for line in range(2):
        for right in range(2):
            image_ref[line, pl.ds(right, cols, stride=2), :] = (
                base + total[line * cols : (line + 1) * cols, right * thin : (right + 1) * thin]
            )


def border_stage(place, coarse, above, below, left, right, first, second, image):
    rows, cols, thin = coarse.shape

    def whole(array):
        zeros = (0,) * array.ndim
        return pl.BlockSpec(array.shape, lambda i: zeros, pipeline_mode=pl.Buffered(1))

    arrays = (above, below, left, right, first, second)
    return pl.pallas_call(
        border_kernel,
        grid=(2,),
        out_shape=jax.ShapeDtypeStruct(image.shape, F32),
        in_specs=[SM, pl.BlockSpec((2, cols, thin), lambda i: (i * (rows // 2 - 1), 0, 0))]
        + [whole(array) for array in arrays]
        + [pl.BlockSpec(memory_space=pl.ANY)],
        out_specs=pl.BlockSpec((2, 2 * cols, thin), lambda i: (i * (rows - 1), 0, 0)),
        input_output_aliases={8: 0},
        compiler_params=PARAMS,
        name="border_stage",
    )(place, coarse, *arrays, image)


def per_device(
    codes,
    starts,
    embed,
    gain_one,
    row_qkv,
    row_out,
    gain_two,
    col_qkv,
    col_out,
    gain_three,
    mlp_in,
    mlp_out,
    project,
    conv_one,
    conv_two,
):
    rows, cols = codes.shape
    _, width = embed.shape
    row_devices = lax.axis_size("row")
    col_devices = lax.axis_size("col")
    row_index = lax.axis_index("row")
    col_index = lax.axis_index("col")

    blocks = [codes]
    for hop in range(1, col_devices):
        ahead = [(i, i + hop) for i in range(col_devices - hop)]
        blocks.insert(0, lax.ppermute(codes, "col", ahead))
    query_table, pair_table = table_stage(embed, gain_one[None, :], row_qkv)
    ends = jnp.stack(
        [row_index, row_devices - 1 - row_index, col_index, col_devices - 1 - col_index]
    ).astype(jnp.int32)
    first_weights, second_weights = weights_stage(conv_one, conv_two)

    part = rows // CHUNKS
    hops = row_devices // 2

    def ahead(step):
        return [(i, i + step) for i in range(row_devices - step)]

    def spread(block, direct):
        held = [block]
        for hop in range(1, hops):
            if hop <= 2 or (direct and hop == 3):
                held.append(lax.ppermute(block, "row", ahead(2 * hop)))
            else:
                held.append(lax.ppermute(held[-1], "row", ahead(2)))
        swap = [(i, i ^ 1) for i in range(row_devices)]
        every = []
        for block in held:
            every += [block, lax.ppermute(block, "row", swap)]
        return every

    queries, hiddens, pairs = [], [], []
    for chunk in range(CHUNKS):
        split = chunk == CHUNKS - 1
        hidden, query, *pair = row_stage(
            chunk * part,
            part,
            split,
            col_index[None],
            blocks,
            query_table,
            pair_table,
            embed,
            row_out,
            gain_two[None, :],
            col_qkv,
        )
        hiddens.append(hidden.reshape(cols, part, width))
        queries.append(query.reshape(cols, part, width))
        for block in pair:
            block = block.reshape(cols // (1 + split), part, block.shape[1])
            pairs.append(spread(block, split))

    count = cols // 16
    fixed = (row_index[None], starts, col_out, gain_three[None, :], mlp_in, mlp_out, project)
    firm = sum(pairs[:-2], [])
    spread_out = (True,) * len(firm) + (False,) * len(pairs[-1])
    block_out, coarse, top, bottom, first_col, last_col = col_stage(
        queries,
        hiddens,
        firm + pairs[-2],
        spread_out,
        lambda i: i + jnp.where(i < count // 2, 0, count),
        count,
        True,
        (),
        *fixed,
    )

    def along(axis, step):
        size = lax.axis_size(axis)
        return [(i, i + step) for i in range(size) if 0 <= i + step < size]

    left = lax.ppermute(last_col, "col", along("col", 1))
    right = lax.ppermute(first_col, "col", along("col", -1))
    block_out, coarse, top, bottom = col_stage(
        queries,
        hiddens,
        firm + pairs[-1],
        spread_out,
        lambda i: i + count // 2,
        count,
        False,
        (block_out, coarse, top, bottom),
        *fixed,
    )

    def wide(line, row):
        return jnp.concatenate([left[row : row + 1], line, right[row : row + 1]], axis=0)

    above = lax.ppermute(wide(bottom, rows - 1), "row", along("row", 1))
    below = lax.ppermute(wide(top, 0), "row", along("row", -1))
    image = conv_stage(
        ends, coarse, left, right, first_col, last_col, first_weights, second_weights
    )
    image = border_stage(
        ends, coarse, above, below, left, right, first_weights, second_weights, image
    )
    return (block_out, image)


def solution(mesh):
    in_specs = (P("row", "col"),) + (P(),) * 14
    out_specs = (P("row", "col", None), P("row", "col", None))
    return jax.shard_map(
        per_device, mesh=mesh, in_specs=in_specs, out_specs=out_specs, check_vma=False
    )
```

```python
import functools
import jax
import jax.numpy as jnp
from jax import lax
from jax.experimental import pallas as pl
from jax.experimental.pallas import tpu as pltpu
from jax.sharding import PartitionSpec as P

HEADS = 8
CHUNKS = 2
EPS = 1e-06
NEGATIVE = -1e30
BF = jnp.bfloat16
F32 = jnp.float32
VM = pl.BlockSpec(memory_space=pltpu.VMEM)
ANY = pl.BlockSpec(memory_space=pl.ANY)
SM = pl.BlockSpec(memory_space=pltpu.SMEM)
PARAMS = pltpu.CompilerParams(vmem_limit_bytes=56 * 1024 * 1024)


def dot(left, right):
    return jnp.dot(left, right, preferred_element_type=F32)


def dot_t(left, right):
    return lax.dot_general(left, right, (((1,), (1,)), ((), ())), preferred_element_type=F32)


def norm_round(values, norm_gain):
    scale = lax.rsqrt(jnp.mean(values * values, axis=-1, keepdims=True) + EPS)
    return (values * scale * norm_gain).astype(BF)


def silu(values):
    return values / (1.0 + jnp.exp(-values))


def one_hot(ids, vocab):
    ids = jnp.concatenate([ids] * (vocab // ids.shape[1]), axis=1)
    spots = lax.broadcasted_iota(jnp.int32, ids.shape, 1)
    spots = (spots - vocab // 2).astype(F32).astype(BF)
    return jnp.where(ids == spots, jnp.ones_like(ids), jnp.zeros_like(ids))


def low_half(shape):
    return lax.broadcasted_iota(jnp.int32, shape, len(shape) - 1) % 128 < 64


def table_kernel(embed_ref, gain_ref, row_qkv_ref, query_ref, pair_ref):
    width = embed_ref.shape[1]
    normed = norm_round(embed_ref[...].astype(F32), gain_ref[...])
    scale = jnp.asarray((width // HEADS) ** (-0.5), BF)
    query_ref[...] = dot(normed, row_qkv_ref[:, :width]).astype(BF) * scale
    for part in range(2):
        found = dot(normed, row_qkv_ref[:, (part + 1) * width : (part + 2) * width])
        pair_ref[part * width : (part + 1) * width, :] = found.T.astype(BF)


def table_stage(embed, gain, row_qkv):
    vocab, width = embed.shape
    return pl.pallas_call(
        table_kernel,
        out_shape=(
            jax.ShapeDtypeStruct((vocab, width), BF),
            jax.ShapeDtypeStruct((2 * width, vocab), BF),
        ),
        in_specs=[VM] * 3,
        out_specs=(VM, VM),
        compiler_params=PARAMS,
        name="table_stage",
    )(embed, gain, row_qkv)


def row_kernel(first, rows, split, block_count, *refs):
    place_ref = refs[0]
    blocks = refs[1 : 1 + block_count]
    (
        query_table_ref,
        pair_table_ref,
        embed_ref,
        row_out_ref,
        gain_ref,
        col_qkv_ref,
        hidden_ref,
        query_ref,
        *targets,
        outward_ref,
        col_ref,
        hidden_held,
        query_held,
        in_sems,
        out_sems,
        mixed_ref,
        queries_ref,
        chosen_ref,
        bias_ref,
        pairs_a,
        pairs_b,
        pairs_c,
        raised_a,
        raised_b,
        raised_c,
    ) = refs[1 + block_count :]
    pair_refs = (pairs_a, pairs_b, pairs_c)
    raised_refs = (raised_a, raised_b, raised_c)
    vocab, width = query_table_ref.shape
    cols = blocks[0].shape[1]
    keys = cols * block_count
    tiles = width // 128
    half = vocab // 2
    loads = [
        pltpu.make_async_copy(embed_ref, outward_ref.at[0:vocab], in_sems.at[0]),
        pltpu.make_async_copy(row_out_ref, outward_ref.at[vocab : vocab + width], in_sems.at[1]),
        pltpu.make_async_copy(col_qkv_ref, col_ref, in_sems.at[2]),
    ]
    for load in loads:
        load.start()

    own = (blocks[-1][first : first + rows, :] - half).astype(F32)
    lines = lax.broadcasted_iota(jnp.int32, (cols, cols), 0)
    lanes = lax.broadcasted_iota(jnp.int32, (cols, cols), 1)
    identity = jnp.where(lines == lanes, 1.0, 0.0).astype(BF)
    turned = dot_t(identity, own.astype(BF))
    for row in range(rows):
        ids = jnp.broadcast_to(turned[:, row : row + 1], (cols, 128)).astype(BF)
        chosen_ref[row * cols : (row + 1) * cols, :] = one_hot(ids, vocab)
    queries_ref[...] = dot(chosen_ref[...], query_table_ref[...]).astype(BF)
    for column in range(cols):
        ids = jnp.broadcast_to(own[:, column : column + 1], (rows, 128)).astype(BF)
        chosen_ref[column * rows : (column + 1) * rows, :] = one_hot(ids, vocab)
    line = lax.broadcasted_iota(jnp.int32, (cols, keys), 0)
    key = lax.broadcasted_iota(jnp.int32, (cols, keys), 1) - (block_count - 1) * cols
    visible = (key <= line) & (key >= -place_ref[2] * cols)
    bias = jnp.where(visible, 0.0, NEGATIVE)
    bias_ref[0:cols, :] = bias
    bias_ref[cols : 2 * cols, :] = bias

    spots = (lax.broadcasted_iota(jnp.int32, (vocab, keys), 0) - half).astype(F32).astype(BF)
    low = low_half((cols, 128))
    ones = jnp.ones((128, keys), BF)

    def gather(row, into):
        row = jnp.minimum(row, rows - 1) + first
        ids = jnp.concatenate([block[pl.ds(row, 1), :] for block in blocks], axis=1)
        ids = (ids - half).astype(F32).astype(BF)
        ids = jnp.broadcast_to(ids, (vocab, keys))
        chosen = jnp.where(ids == spots, jnp.ones_like(ids), jnp.zeros_like(ids))
        into[...] = dot(pair_table_ref[...], chosen).astype(BF)

    def score(row, source, into):
        row = jnp.clip(row, 0, rows - 1)
        for tile in range(tiles):
            here = slice(tile * 128, (tile + 1) * 128)
            query = queries_ref[pl.ds(pl.multiple_of(row * cols, cols), cols), here]
            none = jnp.zeros_like(query)
            query = jnp.concatenate([jnp.where(low, query, none), jnp.where(low, none, query)], axis=0)
            scores = dot(query, source[here, :]) + bias_ref[...]
            into[here, :] = jnp.exp(scores - jnp.max(scores, axis=1, keepdims=True)).astype(BF)

    def mix(row, source, values):
        row = jnp.maximum(row, 0)
        for tile in range(tiles):
            here = slice(tile * 128, (tile + 1) * 128)
            value = values[width + tile * 128 : width + (tile + 1) * 128, :]
            found = dot_t(source[here, :], jnp.concatenate([value, ones], axis=0))
            top = jnp.where(low, found[:cols, :128], found[cols:, :128])
            total = jnp.where(low, found[:cols, 128:], found[cols:, 128:])
            mixed_ref[tile, pl.ds(row, cols, stride=rows), :] = top / total

    def steps(turn, carry):
        for slot in range(3):
            row = 3 * turn + slot
            gather(row, pair_refs[slot])
            score(row - 1, pair_refs[(slot - 1) % 3], raised_refs[slot])
            mix(row - 2, raised_refs[(slot - 1) % 3], pair_refs[(slot - 2) % 3])
        return carry

    lax.fori_loop(0, pl.cdiv(rows + 2, 3), steps, 0)

    for load in loads:
        load.wait()
    step = rows * cols // 2
    stores = []
    for block in range(2):
        here = slice(block * step, (block + 1) * step)
        mixed = [mixed_ref[tile, here, :].astype(BF) for tile in range(tiles)]
        hidden = dot(
            jnp.concatenate([chosen_ref[here, :]] + mixed, axis=1),
            outward_ref[...],
        )
        hidden_held[here, :] = hidden
        projected = dot(norm_round(hidden, gain_ref[...]), col_ref[...]).astype(BF)
        query_held[here, :] = projected[:, :width] * jnp.asarray((width // HEADS) ** (-0.5), BF)
        stores += [
            pltpu.make_async_copy(hidden_held.at[here], hidden_ref.at[here], out_sems.at[0, block]),
            pltpu.make_async_copy(query_held.at[here], query_ref.at[here], out_sems.at[1, block]),
        ]
        for store in stores[-2:]:
            store.start()
        pair = projected[:, width:]
        if split:
            near, far = pair[: step // 2], pair[step // 2 :]
            outer, inner = (near, far) if block == 0 else (far, near)
            spot = slice(block * (step // 2), (block + 1) * (step // 2))
            targets[0][spot, :] = outer
            targets[1][spot, :] = inner
        else:
            targets[0][here, :] = pair
    for store in stores:
        store.wait()


def row_stage(first, rows, split, place, blocks, query_table, pair_table, embed, row_out, gain, col_qkv):
    cols = blocks[0].shape[1]
    keys = cols * len(blocks)
    cells = rows * cols
    vocab, width = embed.shape
    return pl.pallas_call(
        functools.partial(row_kernel, first, rows, split, len(blocks)),
        out_shape=(
            jax.ShapeDtypeStruct((cells, width), F32),
            jax.ShapeDtypeStruct((cells, width), BF),
        )
        + (jax.ShapeDtypeStruct((cells // (1 + split), col_qkv.shape[1] - width), BF),) * (1 + split),
        in_specs=[SM] + [VM] * (len(blocks) + 2) + [ANY, ANY, VM, ANY],
        out_specs=(ANY, ANY) + (VM,) * (1 + split),
        scratch_shapes=[
            pltpu.VMEM((vocab + width, width), BF),
            pltpu.VMEM(col_qkv.shape, BF),
            pltpu.VMEM((cells, width), F32),
            pltpu.VMEM((cells, width), BF),
            pltpu.SemaphoreType.DMA((3,)),
            pltpu.SemaphoreType.DMA((2, 2)),
            pltpu.VMEM((width // 128, cells, 128), F32),
            pltpu.VMEM((cells, width), BF),
            pltpu.VMEM((cells, vocab), BF),
            pltpu.VMEM((2 * cols, keys), F32),
        ]
        + [pltpu.VMEM((2 * width, keys), BF)] * 3
        + [pltpu.VMEM((width, keys), BF)] * 3,
        compiler_params=PARAMS,
        name="row_stage",
    )(place, *blocks, query_table, pair_table, embed, row_out, gain, col_qkv)


def col_kernel(chunks, hops, edges, alias, *refs):
    blocks = 2 * hops * chunks
    queries = refs[:chunks]
    hiddens = refs[chunks : 2 * chunks]
    pairs = refs[2 * chunks : 2 * chunks + blocks]
    (
        place_ref,
        starts_ref,
        gain_ref,
        *rest,
    ) = refs[2 * chunks + blocks :]
    sources = rest[:4]
    rest = rest[8:] if alias else rest[4:]
    block_ref, coarse_ref, top_ref, bottom_ref = rest[:4]
    sides = rest[4:6] if edges else None
    (
        wide_ref,
        thin_ref,
        mixed_ref,
        bias_ref,
        raised_ref,
        turned_ref,
        hidden_ref,
        normed_ref,
        inner_ref,
        col_out_ref,
        mlp_in_ref,
        mlp_out_ref,
        project_ref,
        sems,
    ) = rest[6 if edges else 4 :]
    held = (col_out_ref, mlp_in_ref, mlp_out_ref, project_ref)
    loads = [
        pltpu.make_async_copy(source, target, sems.at[i])
        for i, (source, target) in enumerate(zip(sources, held))
    ]
    group, part, width = queries[0].shape
    rows = part * chunks
    tiles = width // 128
    keys = part * blocks
    index = pl.program_id(0)
    low = low_half((rows, 128))
    low_keys = low_half((keys, 128))

    @pl.when(index == 0)
    def _():
        for load in loads:
            load.start()
        place = place_ref[0]
        lane = lax.broadcasted_iota(jnp.int32, (8, keys), 1)
        spot = lane
        for chunk in range(chunks):
            for hop in range(hops):
                for other in range(2):
                    device = (place if other == 0 else place + 1 - 2 * (place % 2)) - 2 * hop
                    block = (chunk * hops + hop) * 2 + other
                    shift = device * rows + (chunk - block) * part
                    spot = jnp.where(lane // part == block, lane + shift, spot)
        for row in range(rows):
            query_row = place * rows + row
            start = starts_ref[query_row]
            visible = (spot >= start) & (spot <= query_row)
            bias_ref[row : row + 1, :] = jnp.where(visible, 0.0, NEGATIVE)[:1]

    def raise_scores(column):
        query = jnp.concatenate([piece[column] for piece in queries], axis=0)
        none = jnp.zeros((rows, 128), BF)
        evens, odds = [], []
        for tile in range(tiles):
            piece = query[:, tile * 128 : (tile + 1) * 128]
            evens.append(jnp.where(low, piece, none))
            odds.append(jnp.where(low, none, piece))
        pair = jnp.concatenate([piece[column] for piece in pairs], axis=0)
        turned = jnp.concatenate([pair[:, 64:], pair[:, :64]], axis=1)
        turned_ref[column % 3] = turned
        bias = jnp.concatenate([bias_ref[...]] * tiles, axis=0)
        for side, (pieces, key) in enumerate(((evens, pair), (odds, turned))):
            scores = dot_t(jnp.concatenate(pieces, axis=0), key) + bias
            raised = jnp.exp(scores - jnp.max(scores, axis=1, keepdims=True))
            raised_ref[column % 3, side] = raised.astype(BF)

    def mix(column):
        pair = jnp.concatenate([piece[column] for piece in pairs], axis=0)
        turned = turned_ref[column % 3]
        ones = jnp.ones((keys, 128), BF)
        values = (jnp.where(low_keys, turned, ones), jnp.where(low_keys, ones, pair))
        founds = [dot(raised_ref[column % 3, side], value) for side, value in enumerate(values)]
        for tile in range(tiles):
            here = slice(tile * rows, (tile + 1) * rows)
            even, odd = founds[0][here], founds[1][here]
            total = pltpu.roll(jnp.where(low, odd, even), 64, 1)
            mixed = jnp.where(low, even, odd) / total
            mixed_ref[column * rows : (column + 1) * rows, tile * 128 : (tile + 1) * 128] = mixed.astype(BF)

    def begin():
        hidden = jnp.concatenate(
            [piece[column] for column in range(group) for piece in hiddens], axis=0
        )
        hidden = hidden + dot(mixed_ref[...], col_out_ref[...])
        hidden_ref[...] = hidden
        normed_ref[...] = norm_round(hidden, gain_ref[...])

    inner_parts = mlp_in_ref.shape[1] // 4

    def feed_in(piece):
        here = slice(piece * inner_parts, (piece + 1) * inner_parts)
        inner_ref[:, here] = silu(dot(normed_ref[...], mlp_in_ref[:, here])).astype(BF)

    def feed_out(piece):
        half = width // 2
        here = slice(piece * half, (piece + 1) * half)
        block_out = hidden_ref[:, here] + dot(inner_ref[...], mlp_out_ref[:, here])
        normed_ref[:, here] = block_out.astype(BF)
        for column in range(group):
            lines = slice(column * rows, (column + 1) * rows)
            for tile in range(half // 128):
                wide_ref[piece * (half // 128) + tile, pl.ds(column, rows, stride=group), :] = (
                    block_out[lines, tile * 128 : (tile + 1) * 128]
                )

    def finish():
        coarse = dot(normed_ref[...], project_ref[...]).astype(BF).astype(F32)
        for column in range(group):
            thin_ref[pl.ds(column, rows, stride=group), :] = coarse[column * rows : (column + 1) * rows]
        if edges:
            sides[0][...] = jnp.where(index == 1, coarse[:rows], sides[0][...])
            sides[1][...] = coarse[(group - 1) * rows :]
        coarse_ref[...] = thin_ref[...].reshape(coarse_ref.shape)
        top_ref[...] = thin_ref[0:group, :]
        bottom_ref[...] = thin_ref[(rows - 1) * group : rows * group, :]
        for tile in range(tiles):
            block_ref[:, :, tile * 128 : (tile + 1) * 128] = wide_ref[tile].reshape(rows, group, 128)

    feed = [functools.partial(feed_in, piece) for piece in range(4)]
    feed += [functools.partial(feed_out, piece) for piece in range(2)]
    feed += [finish]
    last = pl.num_programs(0) - 1

    def attend(between):
        for column in range(2):
            raise_scores(column)
        for column in range(group):
            if column + 2 < group:
                raise_scores(column + 2)
            if column < len(between):
                between[column]()
            mix(column)

    @pl.when(index == 0)
    def _():
        attend([])

    @pl.when(index == 1)
    def _():
        for load in loads:
            load.wait()

    @pl.when((index > 0) & (index < last))
    def _():
        begin()
        attend(feed)

    @pl.when(index == last)
    def _():
        begin()
        for piece in feed:
            piece()


def col_stage(queries, hiddens, pairs, whole_pairs, places, count, edges, previous, place, starts, *fixed):
    group = 8
    chunks = len(queries)
    hops = len(pairs) // (2 * chunks)
    cols, part_rows, width = queries[0].shape
    rows = part_rows * chunks
    keys = part_rows * len(pairs)
    thin = fixed[-1].shape[1]

    def now(i):
        return jnp.minimum(i, count - 1)

    def late(i):
        return jnp.maximum(i - 1, 0)

    def by_column(array, which):
        return pl.BlockSpec((group,) + array.shape[1:], lambda i: (which(i), 0, 0))

    def whole(array):
        return pl.BlockSpec(array.shape, lambda i: (0, 0), pipeline_mode=pl.Buffered(1))

    placed_now = lambda i: places(now(i))
    placed_late = lambda i: places(late(i))
    pair_specs = [
        by_column(array, placed_now if spread else now) for array, spread in zip(pairs, whole_pairs)
    ]
    out_shape = [
        jax.ShapeDtypeStruct((rows, cols, width), F32),
        jax.ShapeDtypeStruct((rows, cols, thin), F32),
        jax.ShapeDtypeStruct((cols, thin), F32),
        jax.ShapeDtypeStruct((cols, thin), F32),
    ]
    out_specs = [
        pl.BlockSpec((rows, group, width), lambda i: (0, placed_late(i), 0)),
        pl.BlockSpec((rows, group, thin), lambda i: (0, placed_late(i), 0)),
        pl.BlockSpec((group, thin), lambda i: (placed_late(i), 0)),
        pl.BlockSpec((group, thin), lambda i: (placed_late(i), 0)),
    ]
    if edges:
        out_shape += [jax.ShapeDtypeStruct((rows, thin), F32)] * 2
        out_specs += [pl.BlockSpec((rows, thin), lambda i: (0, 0))] * 2
    first = len(queries) * 2 + len(pairs) + 2 + len(fixed)
    gain, *weights = fixed
    return pl.pallas_call(
        functools.partial(col_kernel, chunks, hops, edges, bool(previous)),
        grid=(count + 1,),
        out_shape=tuple(out_shape),
        in_specs=[by_column(array, placed_now) for array in queries]
        + [by_column(array, placed_late) for array in hiddens]
        + pair_specs
        + [SM, SM]
        + [whole(gain)]
        + [ANY] * (len(weights) + len(previous)),
        out_specs=tuple(out_specs),
        scratch_shapes=[
            pltpu.VMEM((width // 128, rows * group, 128), F32),
            pltpu.VMEM((rows * group, thin), F32),
            pltpu.VMEM((rows * group, width), BF),
            pltpu.VMEM((rows, keys), F32),
            pltpu.VMEM((3, 2, rows * (width // 128), keys), BF),
            pltpu.VMEM((3, keys, 128), BF),
            pltpu.VMEM((rows * group, width), F32),
            pltpu.VMEM((rows * group, width), BF),
            pltpu.VMEM((rows * group, weights[1].shape[1]), BF),
        ]
        + [pltpu.VMEM(array.shape, BF) for array in weights]
        + [pltpu.SemaphoreType.DMA((len(weights),))],
        input_output_aliases={first + i: i for i in range(len(previous))},
        compiler_params=PARAMS,
        name="col_stage",
    )(*queries, *hiddens, *pairs, place, starts, *fixed, *previous)


def weights_kernel(one_ref, two_ref, first_ref, second_ref):
    thin = one_ref.shape[2]
    none = jnp.zeros((thin, thin), BF)

    def tap(down, right):
        return one_ref[down, right].astype(F32)

    for phase in range(2):
        sums = (((0, 1), (2,)), ((0,), (1, 2)))[phase]
        for low_side in range(2):
            line = [sum(tap(down, right) for down in sums[low_side]) for right in range(3)]
            even = (line[0], line[1] + line[2], None)
            odd = (None, line[0] + line[1], line[2])
            for column in range(3):
                place = (3 * low_side + column) * thin
                for side, value in enumerate((even[column], odd[column])):
                    lane = (2 * phase + side) * thin
                    value = none if value is None else value.astype(BF)
                    first_ref[place : place + thin, lane : lane + thin] = value
    for down in range(3):
        for column in range(4):
            place = column * thin
            even = two_ref[down, column] if column < 3 else none
            odd = two_ref[down, column - 1] if column > 0 else none
            second_ref[down, place : place + thin, 0:thin] = even
            second_ref[down, place : place + thin, thin : 2 * thin] = odd


def weights_stage(one, two):
    thin = one.shape[2]
    return pl.pallas_call(
        weights_kernel,
        out_shape=(
            jax.ShapeDtypeStruct((6 * thin, 4 * thin), BF),
            jax.ShapeDtypeStruct((3, 4 * thin, 2 * thin), BF),
        ),
        in_specs=[VM, VM],
        out_specs=(VM, VM),
        compiler_params=PARAMS,
        name="weights_stage",
    )(one, two)


def conv_kernel(
    place_ref,
    coarse_ref,
    left_ref,
    right_ref,
    own_left_ref,
    own_right_ref,
    first_ref,
    second_ref,
    image_ref,
    near_ref,
    fine_ref,
    edge_ref,
):
    rows, cols, thin = coarse_ref.shape
    lines = image_ref.shape[0]
    index = pl.program_id(0)
    batch = max(n for n in range(1, 12) if (rows + 1) % n == 0)
    spot = lax.broadcasted_iota(jnp.int32, (cols, thin), 0)

    @pl.when(index == 0)
    def _():
        def put(row, carry):
            line = coarse_ref[row]
            before = jnp.where(spot == 0, left_ref[pl.ds(row, 1), :], pltpu.roll(line, 1, 0))
            after = jnp.where(spot == cols - 1, right_ref[pl.ds(row, 1), :], pltpu.roll(line, cols - 1, 0))
            near_ref[row + 1] = jnp.concatenate([before.astype(BF), line.astype(BF), after.astype(BF)], axis=1)
            return carry

        near_ref[0] = jnp.zeros((cols, 3 * thin), BF)
        near_ref[rows + 1] = jnp.zeros((cols, 3 * thin), BF)
        lax.fori_loop(0, rows, put, 0, unroll=4)

        none = jnp.zeros((rows - 1, thin), BF)
        for side in range(2):
            pieces = []
            for offset in range(2):
                here = slice(offset, offset + rows - 1)
                own = (own_left_ref, own_right_ref)[side][here, :].astype(BF)
                other = (left_ref, right_ref)[side][here, :].astype(BF)
                pieces += [none, other, own] if side == 0 else [own, other, none]
            found = silu(dot(jnp.concatenate(pieces, axis=1), first_ref[...]))
            found = found * jnp.where(place_ref[2 + side] == 0, 0.0, 1.0)
            for phase in range(2):
                lane = (2 * phase + 1 - side) * thin
                edge_ref[side, phase, 1:rows, :] = found[:, lane : lane + thin]

        def fill(turn, carry):
            start = turn * batch
            upper = near_ref[pl.ds(start, batch)].reshape(batch * cols, 3 * thin)
            lower = near_ref[pl.ds(start + 1, batch)].reshape(batch * cols, 3 * thin)
            for phase in range(2):
                lanes = slice(2 * phase * thin, 2 * (phase + 1) * thin)
                found = silu(
                    dot(upper, first_ref[: 3 * thin, lanes]) + dot(lower, first_ref[3 * thin :, lanes])
                )
                for row in range(batch):
                    even = found[row * cols : (row + 1) * cols, :thin]
                    odd = found[row * cols : (row + 1) * cols, thin:]
                    edges = [edge_ref[side, phase, pl.ds(start + row, 1), :] for side in range(2)]
                    before = jnp.where(spot == 0, edges[0], pltpu.roll(odd, 1, 0))
                    after = jnp.where(spot == cols - 1, edges[1], pltpu.roll(even, cols - 1, 0))
                    fine_ref[2 * (start + row) + phase] = jnp.concatenate(
                        [before.astype(BF), even.astype(BF), odd.astype(BF), after.astype(BF)], axis=1
                    )
            return carry

        lax.fori_loop(0, (rows + 1) // batch, fill, 0)

    step = 16

    def second_conv(turn, carry):
        start = index * lines + turn * step
        found = jnp.zeros((step * cols, 2 * thin), F32)
        for shift in range(3):
            values = fine_ref[pl.ds(start + shift, step)].reshape(step * cols, 4 * thin)
            found = found + dot(values, second_ref[shift])
        for line in range(step):
            base = coarse_ref[start // 2 + line // 2]
            for right in range(2):
                image_ref[turn * step + line, pl.ds(right, cols, stride=2), :] = (
                    base + found[line * cols : (line + 1) * cols, right * thin : (right + 1) * thin]
                )
        return carry

    lax.fori_loop(0, lines // step, second_conv, 0)


def conv_stage(place, *arrays):
    rows, cols, thin = arrays[0].shape
    steps = 4
    lines = 2 * rows // steps

    def whole(array):
        zeros = (0,) * array.ndim
        return pl.BlockSpec(array.shape, lambda i: zeros, pipeline_mode=pl.Buffered(1))

    return pl.pallas_call(
        conv_kernel,
        grid=(steps,),
        out_shape=jax.ShapeDtypeStruct((2 * rows, 2 * cols, thin), F32),
        in_specs=[SM] + [whole(array) for array in arrays],
        out_specs=pl.BlockSpec((lines, 2 * cols, thin), lambda i: (i, 0, 0)),
        scratch_shapes=[
            pltpu.VMEM((rows + 2, cols, 3 * thin), BF),
            pltpu.VMEM((2 * rows + 2, cols, 4 * thin), BF),
            pltpu.VMEM((2, 2, rows + 8, thin), F32),
        ],
        compiler_params=PARAMS,
        name="conv_stage",
    )(place, *arrays)


def border_kernel(
    place_ref,
    coarse_ref,
    above_ref,
    below_ref,
    left_ref,
    right_ref,
    first_ref,
    second_ref,
    whole_ref,
    image_ref,
):
    rows = left_ref.shape[0]
    _, cols, thin = coarse_ref.shape
    index = pl.program_id(0)
    upper = index == 0
    spot = lax.broadcasted_iota(jnp.int32, (cols, thin), 0)

    def pick(one, two):
        return jnp.where(upper, one, two)

    lines = (
        pick(above_ref[1 : cols + 1, :], coarse_ref[0]),
        pick(coarse_ref[0], coarse_ref[1]),
        pick(coarse_ref[1], below_ref[1 : cols + 1, :]),
    )
    sides = []
    for source, cell in ((left_ref, 0), (right_ref, cols + 1)):
        sides.append(
            (
                pick(above_ref[cell : cell + 1, :], source[rows - 2 : rows - 1, :]),
                pick(source[0:1, :], source[rows - 1 : rows, :]),
                pick(source[1:2, :], below_ref[cell : cell + 1, :]),
            )
        )
    near = []
    for line, left, right in zip(lines, *sides):
        before = jnp.where(spot == 0, left, pltpu.roll(line, 1, 0))
        after = jnp.where(spot == cols - 1, right, pltpu.roll(line, cols - 1, 0))
        near.append(jnp.concatenate([before.astype(BF), line.astype(BF), after.astype(BF)], axis=1))
    values = jnp.concatenate(
        [jnp.concatenate([near[row], near[row + 1]], axis=1) for row in range(2)], axis=0
    )
    found = silu(dot(values, first_ref[...]))
    none = jnp.zeros((1, thin), F32)
    edge = []
    for side in range(2):
        for row in range(2):
            pieces = []
            for offset in range(2):
                own = lines[row + offset][0:1] if side == 0 else lines[row + offset][cols - 1 : cols]
                other = sides[side][row + offset]
                pieces += [none, other, own] if side == 0 else [own, other, none]
            edge.append(jnp.concatenate(pieces, axis=1))
    edge = jnp.concatenate(edge + [jnp.zeros_like(edge[0])] * 4, axis=0).astype(BF)
    edge = silu(dot(edge, first_ref[...]))
    fine = []
    for row in range(2):
        for phase in range(2):
            lane = 2 * phase * thin
            even = found[row * cols : (row + 1) * cols, lane : lane + thin]
            odd = found[row * cols : (row + 1) * cols, lane + thin : lane + 2 * thin]
            left = edge[row : row + 1, lane + thin : lane + 2 * thin]
            right = edge[2 + row : 3 + row, lane : lane + thin]
            left = left * jnp.where(place_ref[2] == 0, 0.0, 1.0)
            right = right * jnp.where(place_ref[3] == 0, 0.0, 1.0)
            before = jnp.where(spot == 0, left, pltpu.roll(odd, 1, 0))
            after = jnp.where(spot == cols - 1, right, pltpu.roll(even, cols - 1, 0))
            line = jnp.concatenate([before, even, odd, after], axis=1)
            if row == phase:
                keep = jnp.where(place_ref[row] == 0, 0.0, 1.0)
                line = line * jnp.where(upper if row == 0 else index == 1, keep, 1.0)
            fine.append(line.astype(BF))
    total = jnp.zeros((2 * cols, 2 * thin), F32)
    for shift in range(3):
        values = jnp.concatenate([fine[shift], fine[shift + 1]], axis=0)
        total = total + dot(values, second_ref[shift])
    base = pick(coarse_ref[0], coarse_ref[1])
    for line in range(2):
        for right in range(2):
            image_ref[line, pl.ds(right, cols, stride=2), :] = (
                base + total[line * cols : (line + 1) * cols, right * thin : (right + 1) * thin]
            )


def border_stage(place, coarse, above, below, left, right, first, second, image):
    rows, cols, thin = coarse.shape

    def whole(array):
        zeros = (0,) * array.ndim
        return pl.BlockSpec(array.shape, lambda i: zeros, pipeline_mode=pl.Buffered(1))

    arrays = (above, below, left, right, first, second)
    return pl.pallas_call(
        border_kernel,
        grid=(2,),
        out_shape=jax.ShapeDtypeStruct(image.shape, F32),
        in_specs=[SM, pl.BlockSpec((2, cols, thin), lambda i: (i * (rows // 2 - 1), 0, 0))]
        + [whole(array) for array in arrays]
        + [pl.BlockSpec(memory_space=pl.ANY)],
        out_specs=pl.BlockSpec((2, 2 * cols, thin), lambda i: (i * (rows - 1), 0, 0)),
        input_output_aliases={8: 0},
        compiler_params=PARAMS,
        name="border_stage",
    )(place, coarse, *arrays, image)


def per_device(
    codes,
    starts,
    embed,
    gain_one,
    row_qkv,
    row_out,
    gain_two,
    col_qkv,
    col_out,
    gain_three,
    mlp_in,
    mlp_out,
    project,
    conv_one,
    conv_two,
):
    rows, cols = codes.shape
    _, width = embed.shape
    row_devices = lax.axis_size("row")
    col_devices = lax.axis_size("col")
    row_index = lax.axis_index("row")
    col_index = lax.axis_index("col")

    ends = jnp.stack(
        [row_index, row_devices - 1 - row_index, col_index, col_devices - 1 - col_index]
    ).astype(jnp.int32)

    blocks = [codes]
    for hop in range(1, col_devices):
        ahead = [(i, i + hop) for i in range(col_devices - hop)]
        blocks.insert(0, lax.ppermute(codes, "col", ahead))
    query_table, pair_table = table_stage(embed, gain_one[None, :], row_qkv)
    first_weights, second_weights = weights_stage(conv_one, conv_two)

    part = rows // CHUNKS
    hops = row_devices // 2

    def ahead(step):
        return [(i, i + step) for i in range(row_devices - step)]

    def spread(block, direct):
        held = [block]
        for hop in range(1, hops):
            if hop <= 2 or (direct and hop == 3):
                held.append(lax.ppermute(block, "row", ahead(2 * hop)))
            else:
                held.append(lax.ppermute(held[-1], "row", ahead(2)))
        swap = [(i, i ^ 1) for i in range(row_devices)]
        every = []
        for block in held:
            every += [block, lax.ppermute(block, "row", swap)]
        return every

    queries, hiddens, pairs = [], [], []
    for chunk in range(CHUNKS):
        split = chunk == CHUNKS - 1
        hidden, query, *pair = row_stage(
            chunk * part,
            part,
            split,
            ends,
            blocks,
            query_table,
            pair_table,
            embed,
            row_out,
            gain_two[None, :],
            col_qkv,
        )
        hiddens.append(hidden.reshape(cols, part, width))
        queries.append(query.reshape(cols, part, width))
        for block in pair:
            block = block.reshape(cols // (1 + split), part, block.shape[1])
            pairs.append(spread(block, split))

    count = cols // 16
    fixed = (ends, starts, gain_three[None, :], col_out, mlp_in, mlp_out, project)
    firm = sum(pairs[:-2], [])
    spread_out = (True,) * len(firm) + (False,) * len(pairs[-1])
    block_out, coarse, top, bottom, first_col, last_col = col_stage(
        queries,
        hiddens,
        firm + pairs[-2],
        spread_out,
        lambda i: i + jnp.where(i < count // 2, 0, count),
        count,
        True,
        (),
        *fixed,
    )

    def along(axis, step):
        size = lax.axis_size(axis)
        return [(i, i + step) for i in range(size) if 0 <= i + step < size]

    left = lax.ppermute(last_col, "col", along("col", 1))
    right = lax.ppermute(first_col, "col", along("col", -1))
    block_out, coarse, top, bottom = col_stage(
        queries,
        hiddens,
        firm + pairs[-1],
        spread_out,
        lambda i: i + count // 2,
        count,
        False,
        (block_out, coarse, top, bottom),
        *fixed,
    )

    def wide(line, row):
        return jnp.concatenate([left[row : row + 1], line, right[row : row + 1]], axis=0)

    above = lax.ppermute(wide(bottom, rows - 1), "row", along("row", 1))
    below = lax.ppermute(wide(top, 0), "row", along("row", -1))
    image = conv_stage(
        ends, coarse, left, right, first_col, last_col, first_weights, second_weights
    )
    image = border_stage(
        ends, coarse, above, below, left, right, first_weights, second_weights, image
    )
    return (block_out, image)


def solution(mesh):
    in_specs = (P("row", "col"),) + (P(),) * 14
    out_specs = (P("row", "col", None), P("row", "col", None))
    return jax.shard_map(
        per_device, mesh=mesh, in_specs=in_specs, out_specs=out_specs, check_vma=False
    )
```

```python
import functools
import jax
import jax.numpy as jnp
from jax import lax
from jax.experimental import pallas as pl
from jax.experimental.pallas import tpu as pltpu
from jax.sharding import PartitionSpec as P

HEADS = 8
CHUNKS = 2
GROUP = 8
EPS = 1e-06
NEGATIVE = -1e30
BF = jnp.bfloat16
F32 = jnp.float32
VM = pl.BlockSpec(memory_space=pltpu.VMEM)
ANY = pl.BlockSpec(memory_space=pl.ANY)
SM = pl.BlockSpec(memory_space=pltpu.SMEM)
PARAMS = pltpu.CompilerParams(vmem_limit_bytes=56 * 1024 * 1024)


def dot(left, right):
    return jnp.dot(left, right, preferred_element_type=F32)


def dot_t(left, right):
    return lax.dot_general(left, right, (((1,), (1,)), ((), ())), preferred_element_type=F32)


def norm_round(values, norm_gain):
    scale = lax.rsqrt(jnp.mean(values * values, axis=-1, keepdims=True) + EPS)
    return (values * scale * norm_gain).astype(BF)


def silu(values):
    return values / (1.0 + jnp.exp(-values))


def one_hot(ids, vocab):
    ids = jnp.concatenate([ids] * (vocab // ids.shape[1]), axis=1)
    spots = lax.broadcasted_iota(jnp.int32, ids.shape, 1)
    spots = (spots - vocab // 2).astype(F32).astype(BF)
    return jnp.where(ids == spots, jnp.ones_like(ids), jnp.zeros_like(ids))


def low_half(shape):
    return lax.broadcasted_iota(jnp.int32, shape, len(shape) - 1) % 128 < 64


def table_kernel(embed_ref, gain_ref, row_qkv_ref, query_ref, pair_ref):
    width = embed_ref.shape[1]
    normed = norm_round(embed_ref[...].astype(F32), gain_ref[...])
    scale = jnp.asarray((width // HEADS) ** (-0.5), BF)
    query_ref[...] = dot(normed, row_qkv_ref[:, :width]).astype(BF) * scale
    for part in range(2):
        found = dot(normed, row_qkv_ref[:, (part + 1) * width : (part + 2) * width])
        pair_ref[part * width : (part + 1) * width, :] = found.T.astype(BF)


def table_stage(embed, gain, row_qkv):
    vocab, width = embed.shape
    return pl.pallas_call(
        table_kernel,
        out_shape=(
            jax.ShapeDtypeStruct((vocab, width), BF),
            jax.ShapeDtypeStruct((2 * width, vocab), BF),
        ),
        in_specs=[VM] * 3,
        out_specs=(VM, VM),
        compiler_params=PARAMS,
        name="table_stage",
    )(embed, gain, row_qkv)


def row_kernel(first, rows, split, block_count, *refs):
    place_ref = refs[0]
    blocks = refs[1 : 1 + block_count]
    (
        query_table_ref,
        pair_table_ref,
        embed_ref,
        row_out_ref,
        gain_ref,
        col_qkv_ref,
        hidden_ref,
        query_ref,
        *targets,
        outward_ref,
        col_ref,
        hidden_held,
        query_held,
        in_sems,
        out_sems,
        mixed_ref,
        queries_ref,
        chosen_ref,
        bias_ref,
        pairs_a,
        pairs_b,
        pairs_c,
        raised_a,
        raised_b,
        raised_c,
    ) = refs[1 + block_count :]
    pair_refs = (pairs_a, pairs_b, pairs_c)
    raised_refs = (raised_a, raised_b, raised_c)
    vocab, width = query_table_ref.shape
    cols = blocks[0].shape[1]
    keys = cols * block_count
    tiles = width // 128
    half = vocab // 2
    loads = [
        pltpu.make_async_copy(embed_ref, outward_ref.at[0:vocab], in_sems.at[0]),
        pltpu.make_async_copy(row_out_ref, outward_ref.at[vocab : vocab + width], in_sems.at[1]),
        pltpu.make_async_copy(col_qkv_ref, col_ref, in_sems.at[2]),
    ]
    for load in loads:
        load.start()

    own = (blocks[-1][first : first + rows, :] - half).astype(F32)
    lines = lax.broadcasted_iota(jnp.int32, (cols, cols), 0)
    lanes = lax.broadcasted_iota(jnp.int32, (cols, cols), 1)
    identity = jnp.where(lines == lanes, 1.0, 0.0).astype(BF)
    turned = dot_t(identity, own.astype(BF))
    for row in range(rows):
        ids = jnp.broadcast_to(turned[:, row : row + 1], (cols, 128)).astype(BF)
        chosen_ref[row * cols : (row + 1) * cols, :] = one_hot(ids, vocab)
    queries_ref[...] = dot(chosen_ref[...], query_table_ref[...]).astype(BF)
    for column in range(cols):
        ids = jnp.broadcast_to(own[:, column : column + 1], (rows, 128)).astype(BF)
        chosen_ref[column * rows : (column + 1) * rows, :] = one_hot(ids, vocab)
    line = lax.broadcasted_iota(jnp.int32, (cols, keys), 0)
    key = lax.broadcasted_iota(jnp.int32, (cols, keys), 1) - (block_count - 1) * cols
    visible = (key <= line) & (key >= -place_ref[2] * cols)
    bias = jnp.where(visible, 0.0, NEGATIVE)
    bias_ref[0:cols, :] = bias
    bias_ref[cols : 2 * cols, :] = bias

    spots = (lax.broadcasted_iota(jnp.int32, (vocab, keys), 0) - half).astype(F32).astype(BF)
    low = low_half((cols, 128))
    ones = jnp.ones((128, keys), BF)

    def gather(row, into):
        row = jnp.minimum(row, rows - 1) + first
        ids = jnp.concatenate([block[pl.ds(row, 1), :] for block in blocks], axis=1)
        ids = (ids - half).astype(F32).astype(BF)
        ids = jnp.broadcast_to(ids, (vocab, keys))
        chosen = jnp.where(ids == spots, jnp.ones_like(ids), jnp.zeros_like(ids))
        into[...] = dot(pair_table_ref[...], chosen).astype(BF)

    def score(row, source, into):
        row = jnp.clip(row, 0, rows - 1)
        for tile in range(tiles):
            here = slice(tile * 128, (tile + 1) * 128)
            query = queries_ref[pl.ds(pl.multiple_of(row * cols, cols), cols), here]
            none = jnp.zeros_like(query)
            query = jnp.concatenate([jnp.where(low, query, none), jnp.where(low, none, query)], axis=0)
            scores = dot(query, source[here, :]) + bias_ref[...]
            into[here, :] = jnp.exp(scores - jnp.max(scores, axis=1, keepdims=True)).astype(BF)

    def mix(row, source, values):
        row = jnp.maximum(row, 0)
        for tile in range(tiles):
            here = slice(tile * 128, (tile + 1) * 128)
            value = values[width + tile * 128 : width + (tile + 1) * 128, :]
            found = dot_t(source[here, :], jnp.concatenate([value, ones], axis=0))
            top = jnp.where(low, found[:cols, :128], found[cols:, :128])
            total = jnp.where(low, found[:cols, 128:], found[cols:, 128:])
            mixed_ref[tile, pl.ds(row, cols, stride=rows), :] = top / total

    def steps(turn, carry):
        for slot in range(3):
            row = 3 * turn + slot
            gather(row, pair_refs[slot])
            score(row - 1, pair_refs[(slot - 1) % 3], raised_refs[slot])
            mix(row - 2, raised_refs[(slot - 1) % 3], pair_refs[(slot - 2) % 3])
        return carry

    lax.fori_loop(0, pl.cdiv(rows + 2, 3), steps, 0)

    for load in loads:
        load.wait()
    step = rows * cols // 2
    stores = []
    for block in range(2):
        here = slice(block * step, (block + 1) * step)
        mixed = [mixed_ref[tile, here, :].astype(BF) for tile in range(tiles)]
        hidden = dot(
            jnp.concatenate([chosen_ref[here, :]] + mixed, axis=1),
            outward_ref[...],
        )
        hidden_held[here, :] = hidden
        projected = dot(norm_round(hidden, gain_ref[...]), col_ref[...]).astype(BF)
        query_held[here, :] = projected[:, :width] * jnp.asarray((width // HEADS) ** (-0.5), BF)
        stores += [
            pltpu.make_async_copy(hidden_held.at[here], hidden_ref.at[here], out_sems.at[0, block]),
            pltpu.make_async_copy(query_held.at[here], query_ref.at[here], out_sems.at[1, block]),
        ]
        for store in stores[-2:]:
            store.start()
        pair = projected[:, width:]
        if split:
            thick = rows * GROUP
            wide = step - thick
            outer, inner = (pair[:thick], pair[thick:]) if block == 0 else (pair[wide:], pair[:wide])
            targets[0][block * thick : (block + 1) * thick, :] = outer
            targets[1][block * wide : (block + 1) * wide, :] = inner
        else:
            targets[0][here, :] = pair
    for store in stores:
        store.wait()


def row_stage(first, rows, split, place, blocks, query_table, pair_table, embed, row_out, gain, col_qkv):
    cols = blocks[0].shape[1]
    keys = cols * len(blocks)
    cells = rows * cols
    vocab, width = embed.shape
    outer = 2 * GROUP * rows
    sizes = (outer, cells - outer) if split else (cells,)
    return pl.pallas_call(
        functools.partial(row_kernel, first, rows, split, len(blocks)),
        out_shape=(
            jax.ShapeDtypeStruct((cells, width), F32),
            jax.ShapeDtypeStruct((cells, width), BF),
        )
        + tuple(jax.ShapeDtypeStruct((size, col_qkv.shape[1] - width), BF) for size in sizes),
        in_specs=[SM] + [VM] * (len(blocks) + 2) + [ANY, ANY, VM, ANY],
        out_specs=(ANY, ANY) + (VM,) * (1 + split),
        scratch_shapes=[
            pltpu.VMEM((vocab + width, width), BF),
            pltpu.VMEM(col_qkv.shape, BF),
            pltpu.VMEM((cells, width), F32),
            pltpu.VMEM((cells, width), BF),
            pltpu.SemaphoreType.DMA((3,)),
            pltpu.SemaphoreType.DMA((2, 2)),
            pltpu.VMEM((width // 128, cells, 128), F32),
            pltpu.VMEM((cells, width), BF),
            pltpu.VMEM((cells, vocab), BF),
            pltpu.VMEM((2 * cols, keys), F32),
        ]
        + [pltpu.VMEM((2 * width, keys), BF)] * 3
        + [pltpu.VMEM((width, keys), BF)] * 3,
        compiler_params=PARAMS,
        name="row_stage",
    )(place, *blocks, query_table, pair_table, embed, row_out, gain, col_qkv)


def col_kernel(chunks, hops, edges, alias, *refs):
    blocks = 2 * hops * chunks
    queries = refs[:chunks]
    hiddens = refs[chunks : 2 * chunks]
    pairs = refs[2 * chunks : 2 * chunks + blocks]
    (
        place_ref,
        starts_ref,
        gain_ref,
        *rest,
    ) = refs[2 * chunks + blocks :]
    sources = rest[:4]
    rest = rest[8:] if alias else rest[4:]
    block_ref, coarse_ref, top_ref, bottom_ref = rest[:4]
    sides = rest[4:6] if edges else None
    (
        wide_ref,
        thin_ref,
        mixed_ref,
        bias_ref,
        raised_ref,
        turned_ref,
        hidden_ref,
        normed_ref,
        inner_ref,
        col_out_ref,
        mlp_in_ref,
        mlp_out_ref,
        project_ref,
        sems,
    ) = rest[6 if edges else 4 :]
    held = (col_out_ref, mlp_in_ref, mlp_out_ref, project_ref)
    loads = [
        pltpu.make_async_copy(source, target, sems.at[i])
        for i, (source, target) in enumerate(zip(sources, held))
    ]
    group, part, width = queries[0].shape
    rows = part * chunks
    tiles = width // 128
    keys = part * blocks
    index = pl.program_id(0)
    low = low_half((rows, 128))
    low_keys = low_half((keys, 128))

    @pl.when(index == 0)
    def _():
        for load in loads:
            load.start()
        place = place_ref[0]
        lane = lax.broadcasted_iota(jnp.int32, (8, keys), 1)
        spot = lane
        for chunk in range(chunks):
            for hop in range(hops):
                for other in range(2):
                    device = (place if other == 0 else place + 1 - 2 * (place % 2)) - 2 * hop
                    block = (chunk * hops + hop) * 2 + other
                    shift = device * rows + (chunk - block) * part
                    spot = jnp.where(lane // part == block, lane + shift, spot)
        for row in range(rows):
            query_row = place * rows + row
            start = starts_ref[query_row]
            visible = (spot >= start) & (spot <= query_row)
            bias_ref[row : row + 1, :] = jnp.where(visible, 0.0, NEGATIVE)[:1]

    def raise_scores(column):
        query = jnp.concatenate([piece[column] for piece in queries], axis=0)
        none = jnp.zeros((rows, 128), BF)
        evens, odds = [], []
        for tile in range(tiles):
            piece = query[:, tile * 128 : (tile + 1) * 128]
            evens.append(jnp.where(low, piece, none))
            odds.append(jnp.where(low, none, piece))
        pair = jnp.concatenate([piece[column] for piece in pairs], axis=0)
        turned = jnp.concatenate([pair[:, 64:], pair[:, :64]], axis=1)
        turned_ref[column % 3] = turned
        bias = jnp.concatenate([bias_ref[...]] * tiles, axis=0)
        for side, (pieces, key) in enumerate(((evens, pair), (odds, turned))):
            scores = dot_t(jnp.concatenate(pieces, axis=0), key) + bias
            raised = jnp.exp(scores - jnp.max(scores, axis=1, keepdims=True))
            raised_ref[column % 3, side] = raised.astype(BF)

    def mix(column):
        pair = jnp.concatenate([piece[column] for piece in pairs], axis=0)
        turned = turned_ref[column % 3]
        ones = jnp.ones((keys, 128), BF)
        values = (jnp.where(low_keys, turned, ones), jnp.where(low_keys, ones, pair))
        founds = [dot(raised_ref[column % 3, side], value) for side, value in enumerate(values)]
        for tile in range(tiles):
            here = slice(tile * rows, (tile + 1) * rows)
            even, odd = founds[0][here], founds[1][here]
            total = pltpu.roll(jnp.where(low, odd, even), 64, 1)
            mixed = jnp.where(low, even, odd) / total
            mixed_ref[column * rows : (column + 1) * rows, tile * 128 : (tile + 1) * 128] = mixed.astype(BF)

    def begin():
        hidden = jnp.concatenate(
            [piece[column] for column in range(group) for piece in hiddens], axis=0
        )
        hidden = hidden + dot(mixed_ref[...], col_out_ref[...])
        hidden_ref[...] = hidden
        normed_ref[...] = norm_round(hidden, gain_ref[...])

    inner_parts = mlp_in_ref.shape[1] // 4

    def feed_in(piece):
        here = slice(piece * inner_parts, (piece + 1) * inner_parts)
        inner_ref[:, here] = silu(dot(normed_ref[...], mlp_in_ref[:, here])).astype(BF)

    def feed_out(piece):
        half = width // 2
        here = slice(piece * half, (piece + 1) * half)
        block_out = hidden_ref[:, here] + dot(inner_ref[...], mlp_out_ref[:, here])
        normed_ref[:, here] = block_out.astype(BF)
        for column in range(group):
            lines = slice(column * rows, (column + 1) * rows)
            for tile in range(half // 128):
                wide_ref[piece * (half // 128) + tile, pl.ds(column, rows, stride=group), :] = (
                    block_out[lines, tile * 128 : (tile + 1) * 128]
                )

    def finish():
        coarse = dot(normed_ref[...], project_ref[...]).astype(BF).astype(F32)
        for column in range(group):
            thin_ref[pl.ds(column, rows, stride=group), :] = coarse[column * rows : (column + 1) * rows]
        if edges:
            sides[0][...] = jnp.where(index == 1, coarse[:rows], sides[0][...])
            sides[1][...] = coarse[(group - 1) * rows :]
        coarse_ref[...] = thin_ref[...].reshape(coarse_ref.shape)
        top_ref[...] = thin_ref[0:group, :]
        bottom_ref[...] = thin_ref[(rows - 1) * group : rows * group, :]
        for tile in range(tiles):
            block_ref[:, :, tile * 128 : (tile + 1) * 128] = wide_ref[tile].reshape(rows, group, 128)

    feed = [functools.partial(feed_in, piece) for piece in range(4)]
    feed += [functools.partial(feed_out, piece) for piece in range(2)]
    feed += [finish]
    last = pl.num_programs(0) - 1

    def attend(between):
        for column in range(2):
            raise_scores(column)
        for column in range(group):
            if column + 2 < group:
                raise_scores(column + 2)
            if column < len(between):
                between[column]()
            mix(column)

    @pl.when(index == 0)
    def _():
        attend([])

    @pl.when(index == 1)
    def _():
        for load in loads:
            load.wait()

    @pl.when((index > 0) & (index < last))
    def _():
        begin()
        attend(feed)

    @pl.when(index == last)
    def _():
        begin()
        for piece in feed:
            piece()


def col_stage(queries, hiddens, pairs, whole_pairs, places, count, edges, previous, place, starts, *fixed):
    group = GROUP
    chunks = len(queries)
    hops = len(pairs) // (2 * chunks)
    cols, part_rows, width = queries[0].shape
    rows = part_rows * chunks
    keys = part_rows * len(pairs)
    thin = fixed[-1].shape[1]

    def now(i):
        return jnp.minimum(i, count - 1)

    def late(i):
        return jnp.maximum(i - 1, 0)

    def by_column(array, which):
        return pl.BlockSpec((group,) + array.shape[1:], lambda i: (which(i), 0, 0))

    def whole(array):
        return pl.BlockSpec(array.shape, lambda i: (0, 0), pipeline_mode=pl.Buffered(1))

    placed_now = lambda i: places(now(i))
    placed_late = lambda i: places(late(i))
    pair_specs = [
        by_column(array, placed_now if spread else now) for array, spread in zip(pairs, whole_pairs)
    ]
    out_shape = [
        jax.ShapeDtypeStruct((rows, cols, width), F32),
        jax.ShapeDtypeStruct((rows, cols, thin), F32),
        jax.ShapeDtypeStruct((cols, thin), F32),
        jax.ShapeDtypeStruct((cols, thin), F32),
    ]
    out_specs = [
        pl.BlockSpec((rows, group, width), lambda i: (0, placed_late(i), 0)),
        pl.BlockSpec((rows, group, thin), lambda i: (0, placed_late(i), 0)),
        pl.BlockSpec((group, thin), lambda i: (placed_late(i), 0)),
        pl.BlockSpec((group, thin), lambda i: (placed_late(i), 0)),
    ]
    if edges:
        out_shape += [jax.ShapeDtypeStruct((rows, thin), F32)] * 2
        out_specs += [pl.BlockSpec((rows, thin), lambda i: (0, 0))] * 2
    first = len(queries) * 2 + len(pairs) + 2 + len(fixed)
    gain, *weights = fixed
    return pl.pallas_call(
        functools.partial(col_kernel, chunks, hops, edges, bool(previous)),
        grid=(count + 1,),
        out_shape=tuple(out_shape),
        in_specs=[by_column(array, placed_now) for array in queries]
        + [by_column(array, placed_late) for array in hiddens]
        + pair_specs
        + [SM, SM]
        + [whole(gain)]
        + [ANY] * (len(weights) + len(previous)),
        out_specs=tuple(out_specs),
        scratch_shapes=[
            pltpu.VMEM((width // 128, rows * group, 128), F32),
            pltpu.VMEM((rows * group, thin), F32),
            pltpu.VMEM((rows * group, width), BF),
            pltpu.VMEM((rows, keys), F32),
            pltpu.VMEM((3, 2, rows * (width // 128), keys), BF),
            pltpu.VMEM((3, keys, 128), BF),
            pltpu.VMEM((rows * group, width), F32),
            pltpu.VMEM((rows * group, width), BF),
            pltpu.VMEM((rows * group, weights[1].shape[1]), BF),
        ]
        + [pltpu.VMEM(array.shape, BF) for array in weights]
        + [pltpu.SemaphoreType.DMA((len(weights),))],
        input_output_aliases={first + i: i for i in range(len(previous))},
        compiler_params=PARAMS,
        name="col_stage",
    )(*queries, *hiddens, *pairs, place, starts, *fixed, *previous)


def weights_kernel(one_ref, two_ref, first_ref, second_ref):
    thin = one_ref.shape[2]
    none = jnp.zeros((thin, thin), BF)

    def tap(down, right):
        return one_ref[down, right].astype(F32)

    for phase in range(2):
        sums = (((0, 1), (2,)), ((0,), (1, 2)))[phase]
        for low_side in range(2):
            line = [sum(tap(down, right) for down in sums[low_side]) for right in range(3)]
            even = (line[0], line[1] + line[2], None)
            odd = (None, line[0] + line[1], line[2])
            for column in range(3):
                place = (3 * low_side + column) * thin
                for side, value in enumerate((even[column], odd[column])):
                    lane = (2 * phase + side) * thin
                    value = none if value is None else value.astype(BF)
                    first_ref[place : place + thin, lane : lane + thin] = value
    for down in range(3):
        for column in range(4):
            place = column * thin
            even = two_ref[down, column] if column < 3 else none
            odd = two_ref[down, column - 1] if column > 0 else none
            second_ref[down, place : place + thin, 0:thin] = even
            second_ref[down, place : place + thin, thin : 2 * thin] = odd


def weights_stage(one, two):
    thin = one.shape[2]
    return pl.pallas_call(
        weights_kernel,
        out_shape=(
            jax.ShapeDtypeStruct((6 * thin, 4 * thin), BF),
            jax.ShapeDtypeStruct((3, 4 * thin, 2 * thin), BF),
        ),
        in_specs=[VM, VM],
        out_specs=(VM, VM),
        compiler_params=PARAMS,
        name="weights_stage",
    )(one, two)


def conv_kernel(
    place_ref,
    coarse_ref,
    left_ref,
    right_ref,
    own_left_ref,
    own_right_ref,
    first_ref,
    second_ref,
    image_ref,
    near_ref,
    fine_ref,
    edge_ref,
):
    rows, cols, thin = coarse_ref.shape
    lines = image_ref.shape[0]
    index = pl.program_id(0)
    batch = max(n for n in range(1, 12) if (rows + 1) % n == 0)
    spot = lax.broadcasted_iota(jnp.int32, (cols, thin), 0)

    @pl.when(index == 0)
    def _():
        def put(row, carry):
            line = coarse_ref[row]
            before = jnp.where(spot == 0, left_ref[pl.ds(row, 1), :], pltpu.roll(line, 1, 0))
            after = jnp.where(spot == cols - 1, right_ref[pl.ds(row, 1), :], pltpu.roll(line, cols - 1, 0))
            near_ref[row + 1] = jnp.concatenate([before.astype(BF), line.astype(BF), after.astype(BF)], axis=1)
            return carry

        near_ref[0] = jnp.zeros((cols, 3 * thin), BF)
        near_ref[rows + 1] = jnp.zeros((cols, 3 * thin), BF)
        lax.fori_loop(0, rows, put, 0, unroll=4)

        none = jnp.zeros((rows - 1, thin), BF)
        for side in range(2):
            pieces = []
            for offset in range(2):
                here = slice(offset, offset + rows - 1)
                own = (own_left_ref, own_right_ref)[side][here, :].astype(BF)
                other = (left_ref, right_ref)[side][here, :].astype(BF)
                pieces += [none, other, own] if side == 0 else [own, other, none]
            found = silu(dot(jnp.concatenate(pieces, axis=1), first_ref[...]))
            found = found * jnp.where(place_ref[2 + side] == 0, 0.0, 1.0)
            for phase in range(2):
                lane = (2 * phase + 1 - side) * thin
                edge_ref[side, phase, 1:rows, :] = found[:, lane : lane + thin]

        def fill(turn, carry):
            start = turn * batch
            upper = near_ref[pl.ds(start, batch)].reshape(batch * cols, 3 * thin)
            lower = near_ref[pl.ds(start + 1, batch)].reshape(batch * cols, 3 * thin)
            for phase in range(2):
                lanes = slice(2 * phase * thin, 2 * (phase + 1) * thin)
                found = silu(
                    dot(upper, first_ref[: 3 * thin, lanes]) + dot(lower, first_ref[3 * thin :, lanes])
                )
                for row in range(batch):
                    even = found[row * cols : (row + 1) * cols, :thin]
                    odd = found[row * cols : (row + 1) * cols, thin:]
                    edges = [edge_ref[side, phase, pl.ds(start + row, 1), :] for side in range(2)]
                    before = jnp.where(spot == 0, edges[0], pltpu.roll(odd, 1, 0))
                    after = jnp.where(spot == cols - 1, edges[1], pltpu.roll(even, cols - 1, 0))
                    fine_ref[2 * (start + row) + phase] = jnp.concatenate(
                        [before.astype(BF), even.astype(BF), odd.astype(BF), after.astype(BF)], axis=1
                    )
            return carry

        lax.fori_loop(0, (rows + 1) // batch, fill, 0)

    step = 16

    def second_conv(turn, carry):
        start = index * lines + turn * step
        found = jnp.zeros((step * cols, 2 * thin), F32)
        for shift in range(3):
            values = fine_ref[pl.ds(start + shift, step)].reshape(step * cols, 4 * thin)
            found = found + dot(values, second_ref[shift])
        for line in range(step):
            base = coarse_ref[start // 2 + line // 2]
            for right in range(2):
                image_ref[turn * step + line, pl.ds(right, cols, stride=2), :] = (
                    base + found[line * cols : (line + 1) * cols, right * thin : (right + 1) * thin]
                )
        return carry

    lax.fori_loop(0, lines // step, second_conv, 0)


def conv_stage(place, *arrays):
    rows, cols, thin = arrays[0].shape
    steps = 4
    lines = 2 * rows // steps

    def whole(array):
        zeros = (0,) * array.ndim
        return pl.BlockSpec(array.shape, lambda i: zeros, pipeline_mode=pl.Buffered(1))

    return pl.pallas_call(
        conv_kernel,
        grid=(steps,),
        out_shape=jax.ShapeDtypeStruct((2 * rows, 2 * cols, thin), F32),
        in_specs=[SM] + [whole(array) for array in arrays],
        out_specs=pl.BlockSpec((lines, 2 * cols, thin), lambda i: (i, 0, 0)),
        scratch_shapes=[
            pltpu.VMEM((rows + 2, cols, 3 * thin), BF),
            pltpu.VMEM((2 * rows + 2, cols, 4 * thin), BF),
            pltpu.VMEM((2, 2, rows + 8, thin), F32),
        ],
        compiler_params=PARAMS,
        name="conv_stage",
    )(place, *arrays)


def border_kernel(
    place_ref,
    coarse_ref,
    above_ref,
    below_ref,
    left_ref,
    right_ref,
    first_ref,
    second_ref,
    whole_ref,
    image_ref,
):
    rows = left_ref.shape[0]
    _, cols, thin = coarse_ref.shape
    index = pl.program_id(0)
    upper = index == 0
    spot = lax.broadcasted_iota(jnp.int32, (cols, thin), 0)

    def pick(one, two):
        return jnp.where(upper, one, two)

    lines = (
        pick(above_ref[1 : cols + 1, :], coarse_ref[0]),
        pick(coarse_ref[0], coarse_ref[1]),
        pick(coarse_ref[1], below_ref[1 : cols + 1, :]),
    )
    sides = []
    for source, cell in ((left_ref, 0), (right_ref, cols + 1)):
        sides.append(
            (
                pick(above_ref[cell : cell + 1, :], source[rows - 2 : rows - 1, :]),
                pick(source[0:1, :], source[rows - 1 : rows, :]),
                pick(source[1:2, :], below_ref[cell : cell + 1, :]),
            )
        )
    near = []
    for line, left, right in zip(lines, *sides):
        before = jnp.where(spot == 0, left, pltpu.roll(line, 1, 0))
        after = jnp.where(spot == cols - 1, right, pltpu.roll(line, cols - 1, 0))
        near.append(jnp.concatenate([before.astype(BF), line.astype(BF), after.astype(BF)], axis=1))
    values = jnp.concatenate(
        [jnp.concatenate([near[row], near[row + 1]], axis=1) for row in range(2)], axis=0
    )
    found = silu(dot(values, first_ref[...]))
    none = jnp.zeros((1, thin), F32)
    edge = []
    for side in range(2):
        for row in range(2):
            pieces = []
            for offset in range(2):
                own = lines[row + offset][0:1] if side == 0 else lines[row + offset][cols - 1 : cols]
                other = sides[side][row + offset]
                pieces += [none, other, own] if side == 0 else [own, other, none]
            edge.append(jnp.concatenate(pieces, axis=1))
    edge = jnp.concatenate(edge + [jnp.zeros_like(edge[0])] * 4, axis=0).astype(BF)
    edge = silu(dot(edge, first_ref[...]))
    fine = []
    for row in range(2):
        for phase in range(2):
            lane = 2 * phase * thin
            even = found[row * cols : (row + 1) * cols, lane : lane + thin]
            odd = found[row * cols : (row + 1) * cols, lane + thin : lane + 2 * thin]
            left = edge[row : row + 1, lane + thin : lane + 2 * thin]
            right = edge[2 + row : 3 + row, lane : lane + thin]
            left = left * jnp.where(place_ref[2] == 0, 0.0, 1.0)
            right = right * jnp.where(place_ref[3] == 0, 0.0, 1.0)
            before = jnp.where(spot == 0, left, pltpu.roll(odd, 1, 0))
            after = jnp.where(spot == cols - 1, right, pltpu.roll(even, cols - 1, 0))
            line = jnp.concatenate([before, even, odd, after], axis=1)
            if row == phase:
                keep = jnp.where(place_ref[row] == 0, 0.0, 1.0)
                line = line * jnp.where(upper if row == 0 else index == 1, keep, 1.0)
            fine.append(line.astype(BF))
    total = jnp.zeros((2 * cols, 2 * thin), F32)
    for shift in range(3):
        values = jnp.concatenate([fine[shift], fine[shift + 1]], axis=0)
        total = total + dot(values, second_ref[shift])
    base = pick(coarse_ref[0], coarse_ref[1])
    for line in range(2):
        for right in range(2):
            image_ref[line, pl.ds(right, cols, stride=2), :] = (
                base + total[line * cols : (line + 1) * cols, right * thin : (right + 1) * thin]
            )


def border_stage(place, coarse, above, below, left, right, first, second, image):
    rows, cols, thin = coarse.shape

    def whole(array):
        zeros = (0,) * array.ndim
        return pl.BlockSpec(array.shape, lambda i: zeros, pipeline_mode=pl.Buffered(1))

    arrays = (above, below, left, right, first, second)
    return pl.pallas_call(
        border_kernel,
        grid=(2,),
        out_shape=jax.ShapeDtypeStruct(image.shape, F32),
        in_specs=[SM, pl.BlockSpec((2, cols, thin), lambda i: (i * (rows // 2 - 1), 0, 0))]
        + [whole(array) for array in arrays]
        + [pl.BlockSpec(memory_space=pl.ANY)],
        out_specs=pl.BlockSpec((2, 2 * cols, thin), lambda i: (i * (rows - 1), 0, 0)),
        input_output_aliases={8: 0},
        compiler_params=PARAMS,
        name="border_stage",
    )(place, coarse, *arrays, image)


def per_device(
    codes,
    starts,
    embed,
    gain_one,
    row_qkv,
    row_out,
    gain_two,
    col_qkv,
    col_out,
    gain_three,
    mlp_in,
    mlp_out,
    project,
    conv_one,
    conv_two,
):
    rows, cols = codes.shape
    _, width = embed.shape
    row_devices = lax.axis_size("row")
    col_devices = lax.axis_size("col")
    row_index = lax.axis_index("row")
    col_index = lax.axis_index("col")

    ends = jnp.stack(
        [row_index, row_devices - 1 - row_index, col_index, col_devices - 1 - col_index]
    ).astype(jnp.int32)

    blocks = [codes]
    for hop in range(1, col_devices):
        ahead = [(i, i + hop) for i in range(col_devices - hop)]
        blocks.insert(0, lax.ppermute(codes, "col", ahead))
    query_table, pair_table = table_stage(embed, gain_one[None, :], row_qkv)
    first_weights, second_weights = weights_stage(conv_one, conv_two)

    part = rows // CHUNKS
    hops = row_devices // 2

    def ahead(step):
        return [(i, i + step) for i in range(row_devices - step)]

    def spread(block, direct):
        held = [block]
        for hop in range(1, hops):
            if hop <= 2 or (direct and hop == 3):
                held.append(lax.ppermute(block, "row", ahead(2 * hop)))
            else:
                held.append(lax.ppermute(held[-1], "row", ahead(2)))
        swap = [(i, i ^ 1) for i in range(row_devices)]
        every = []
        for block in held:
            every += [block, lax.ppermute(block, "row", swap)]
        return every

    queries, hiddens, pairs = [], [], []
    for chunk in range(CHUNKS):
        split = chunk == CHUNKS - 1
        hidden, query, *pair = row_stage(
            chunk * part,
            part,
            split,
            ends,
            blocks,
            query_table,
            pair_table,
            embed,
            row_out,
            gain_two[None, :],
            col_qkv,
        )
        hiddens.append(hidden.reshape(cols, part, width))
        queries.append(query.reshape(cols, part, width))
        for block in pair:
            block = block.reshape(-1, part, block.shape[1])
            pairs.append(spread(block, split))

    groups = cols // GROUP
    fixed = (ends, starts, gain_three[None, :], col_out, mlp_in, mlp_out, project)
    firm = sum(pairs[:-2], [])
    spread_out = (True,) * len(firm) + (False,) * len(pairs[-1])
    block_out, coarse, top, bottom, first_col, last_col = col_stage(
        queries,
        hiddens,
        firm + pairs[-2],
        spread_out,
        lambda i: i * (groups - 1),
        2,
        True,
        (),
        *fixed,
    )

    def along(axis, step):
        size = lax.axis_size(axis)
        return [(i, i + step) for i in range(size) if 0 <= i + step < size]

    left = lax.ppermute(last_col, "col", along("col", 1))
    right = lax.ppermute(first_col, "col", along("col", -1))
    block_out, coarse, top, bottom = col_stage(
        queries,
        hiddens,
        firm + pairs[-1],
        spread_out,
        lambda i: i + 1,
        groups - 2,
        False,
        (block_out, coarse, top, bottom),
        *fixed,
    )

    def wide(line, row):
        return jnp.concatenate([left[row : row + 1], line, right[row : row + 1]], axis=0)

    above = lax.ppermute(wide(bottom, rows - 1), "row", along("row", 1))
    below = lax.ppermute(wide(top, 0), "row", along("row", -1))
    image = conv_stage(
        ends, coarse, left, right, first_col, last_col, first_weights, second_weights
    )
    image = border_stage(
        ends, coarse, above, below, left, right, first_weights, second_weights, image
    )
    return (block_out, image)


def solution(mesh):
    in_specs = (P("row", "col"),) + (P(),) * 14
    out_specs = (P("row", "col", None), P("row", "col", None))
    return jax.shard_map(
        per_device, mesh=mesh, in_specs=in_specs, out_specs=out_specs, check_vma=False
    )
```
